512 devices in a mesh: tm: 16 (over x, z_hi, core), contact: 32 (over z_lo, y).
Axes of the slice: x: 4, y: 8, z: 8 (z_hi: 2, z_lo: 4; z = z_hi * 4 + z_lo), core: 2. Of those that a mesh axis runs over, the one named last changes fastest.
Arguments:
- signal: bfloat16 [8, 512, 16384], P(None, 'contact', 'tm'), may hold values from -6 to 6
- fir_taps: bfloat16 [512, 129], P('contact'), may hold values from -0.5 to 0.5
- neighbours: int32 [512, 4], replicated, may hold values from 0 to 511, as said below
- live_mask: int32 [512], replicated, may hold values 0 or 1
- lap_coef: float32 [512], replicated, may hold values from 0.1 to 1
- w_query: bfloat16 [256, 256], replicated, may hold values from -8 to 8
- w_key: bfloat16 [256, 256], replicated, may hold values from -8 to 8
- w_value: bfloat16 [256, 256], replicated, may hold values from -0.375 to 0.375
- w_out: bfloat16 [256, 256], replicated, may hold values from -0.375 to 0.375
- cotangent: bfloat16 [8, 512, 16384], P(None, 'contact', 'tm'), may hold values from -6 to 6
Outputs:
- attended: bfloat16 [8, 512, 16384], P(None, 'contact', 'tm')
- weight_grads: float32 [4, 256, 256], replicated
The draws below stay inside these ranges and needn't reach their ends.
Inputs may be any that keep to these rules, and one draw needn't show every extreme that they name: `neighbours`: entry [c, k] names a contact whose grid row (index // 16) differs from that of contact c by at most one and whose column (index % 16) differs by at most two.
All inputs are finite; a program needn't handle non-finite values.
Results may differ from the reference program's by a relative error of at most 0.011.
Values may be sent and summed in bfloat16 or wider, within the bound.
A program may use at most 64 MiB of HBM per device.

```python
import math
import jax
import jax.numpy as jnp
from jax import lax

GRID_ROWS = 32
GRID_COLS = 16
CONTACTS = 512
NEIGHBOURS = 4
TAPS = 129
PATCH = 256
HEADS = 4
BATCH = 8
PATCHES = 64
SAMPLES = 16384


def projection(key, salt):
    matrix = jax.random.normal(jax.random.fold_in(key, salt), (PATCH, PATCH), jnp.float32) / math.sqrt(PATCH)
    return matrix


def draw_w_query(key, part):
    return projection(key, 1).astype(jnp.bfloat16)


def draw_w_key(key, part):
    return projection(key, 2).astype(jnp.bfloat16)


def draw_neighbours(key, part):
    contact_ids = jnp.arange(CONTACTS, dtype=jnp.int32)
    grid_row = contact_ids // GRID_COLS
    grid_col = contact_ids % GRID_COLS
    row_step = jax.random.randint(jax.random.fold_in(key, 21), (CONTACTS, NEIGHBOURS), -1, 2, dtype=jnp.int32)
    col_step = jax.random.randint(jax.random.fold_in(key, 22), (CONTACTS, NEIGHBOURS), -2, 3, dtype=jnp.int32)
    near_row = jnp.clip(grid_row[:, None] + row_step, 0, GRID_ROWS - 1)
    near_col = jnp.clip(grid_col[:, None] + col_step, 0, GRID_COLS - 1)
    return (near_row * GRID_COLS + near_col).astype(jnp.int32)


def touch_ends(drawn, key, smallest, largest):
    spot = [jax.random.randint(jax.random.fold_in(key, axis), (), 0, length) for axis, length in enumerate(drawn.shape)]
    widest = drawn.shape.index(max(drawn.shape))
    next_to = spot[:widest] + [(spot[widest] + 1) % drawn.shape[widest]] + spot[widest + 1:]
    return drawn.at[tuple(spot)].set(smallest).at[tuple(next_to)].set(largest)


def levels(key, shape, split, least, top_value):
    def one(axis_at, shards_of):
        steps = jax.random.uniform(jax.random.fold_in(jax.random.fold_in(key, 6), axis_at), (shards_of,), jnp.float32, least / len(split), top_value / len(split))
        return jnp.repeat(jnp.exp(steps), shape[axis_at] // shards_of).reshape((-1,) + (1,) * (len(shape) - axis_at - 1))

    level = one(*split[0])
    for cut in split[1:]:
        level = level * one(*cut)
    return level


def scatter_about(stream_key, extent, width, limit, pieces=(), kind=jnp.bfloat16):
    entries = jax.random.normal(stream_key, extent, jnp.float32) * width
    if len(pieces) > 0:
        entries = levels(stream_key, extent, pieces, -0.22, 0.18) * entries
    return jnp.clip(entries, min=-limit, max=limit).astype(kind)


def setup_inputs(seed: int = 0) -> dict:
    key_of = jax.random.split(jax.random.key(seed), 11)
    signal = scatter_about(key_of[0], (BATCH, CONTACTS, SAMPLES), 1.0, 6.0, ((1, 32), (2, 16)))
    fir_taps = scatter_about(key_of[1], (CONTACTS, TAPS), TAPS ** -0.5, 0.5, ((0, 32),))
    neighbours = draw_neighbours(jax.random.fold_in(key_of[10], 71), 0)
    live_mask = touch_ends((jax.random.randint(key_of[3], (CONTACTS,), 0, 16) < 15).astype(jnp.int32), jax.random.fold_in(key_of[3], 1), 0, 1)
    lap_coef = jnp.clip(jnp.exp(jax.random.uniform(key_of[4], (CONTACTS,), jnp.float32, math.log(0.1), math.log(1.0))), 0.1, 1.0)
    w_query = draw_w_query(jax.random.fold_in(key_of[10], 71), 0)
    w_key = draw_w_key(jax.random.fold_in(key_of[10], 71), 0)
    w_value = scatter_about(key_of[7], (PATCH, PATCH), PATCH ** -0.5, 0.375)
    w_out = scatter_about(key_of[8], (PATCH, PATCH), PATCH ** -0.5, 0.375)
    cotangent = scatter_about(key_of[9], (BATCH, CONTACTS, SAMPLES), 1.0, 6.0, ((1, 32), (2, 16)))
    return {"signal": signal, "fir_taps": fir_taps, "neighbours": neighbours, "live_mask": live_mask, "lap_coef": lap_coef, "w_query": w_query, "w_key": w_key, "w_value": w_value, "w_out": w_out, "cotangent": cotangent}


def contract(left, right, left_dim, right_dim):
    return lax.dot_general(left, right, (((left_dim,), (right_dim,)), ((), ())), preferred_element_type=jnp.float32)

def toeplitz(fir_taps):
    rim_width = fir_taps.shape[1] - 1
    source = jnp.arange(2 * rim_width, dtype=jnp.int32)[:, None]
    target = jnp.arange(rim_width, dtype=jnp.int32)[None, :]
    lag_table = (target + rim_width - source).astype(jnp.int32)
    inside = (lag_table >= 0) & (lag_table <= rim_width)
    picked = jnp.take(fir_taps, jnp.clip(lag_table, 0, rim_width).astype(jnp.int32), axis=1)
    return jnp.where(inside[None, :, :], picked, jnp.zeros_like(picked))

def laplace(field, centre, indices, nbr_alive, own_alive, coef):
    middle = centre.astype(jnp.float32)
    running = jnp.zeros_like(middle)
    for slot_index in range(indices.shape[1]):
        nearby = jnp.take(field, indices[:, slot_index], axis=-2).astype(jnp.float32)
        running = running + nbr_alive[:, slot_index][:, None] * (nearby - middle)
    return (own_alive[:, None] * (middle + coef[:, None] * running)).astype(jnp.bfloat16)

def one_head(query_head, key_head, value_head, back_head, key_alive, score_scale):
    scores = contract(query_head, key_head, 1, 1) * score_scale
    scores = jnp.where(key_alive[None, :] > 0, scores, -1e+30)
    top_score = lax.optimization_barrier(jnp.max(scores, axis=1, keepdims=True))
    raised = jnp.exp(scores - top_score)
    attn_prob = raised / lax.optimization_barrier(jnp.sum(raised, axis=1, keepdims=True))
    prob_low = attn_prob.astype(jnp.bfloat16)
    head_out = jnp.dot(prob_low, value_head, preferred_element_type=jnp.float32).astype(jnp.bfloat16)
    grad_value = contract(prob_low, back_head, 0, 0).astype(jnp.bfloat16)
    grad_prob = contract(back_head, value_head, 1, 1)
    row_inner = lax.optimization_barrier(jnp.sum(back_head.astype(jnp.float32) * head_out.astype(jnp.float32), axis=1, keepdims=True))
    grad_score = (attn_prob * (grad_prob - row_inner) * score_scale).astype(jnp.bfloat16)
    grad_query = jnp.dot(grad_score, key_head, preferred_element_type=jnp.float32).astype(jnp.bfloat16)
    grad_key = contract(grad_score, query_head, 0, 0).astype(jnp.bfloat16)
    return (head_out, grad_query, grad_key, grad_value)

def group_step(tokens, upstream, key_alive, w_query, w_key, w_value, w_out):
    as_float = tokens.astype(jnp.float32)
    normed = (as_float * lax.rsqrt(lax.optimization_barrier(jnp.mean(as_float * as_float, axis=1, keepdims=True)) + 1e-05)).astype(jnp.bfloat16)
    query_rows = jnp.dot(normed, w_query, preferred_element_type=jnp.float32).astype(jnp.bfloat16)
    key_rows = jnp.dot(normed, w_key, preferred_element_type=jnp.float32).astype(jnp.bfloat16)
    value_rows = jnp.dot(normed, w_value, preferred_element_type=jnp.float32).astype(jnp.bfloat16)
    back_signal = contract(upstream, w_out, 1, 1).astype(jnp.bfloat16)
    head_size = w_query.shape[1] // HEADS
    score_scale = head_size ** (-0.5)
    head_results = []
    for head_index in range(HEADS):
        lower = head_index * head_size
        upper = lower + head_size
        head_results.append(one_head(query_rows[:, lower:upper], key_rows[:, lower:upper], value_rows[:, lower:upper], back_signal[:, lower:upper], key_alive, score_scale))
    mixed_heads = jnp.concatenate([entry[0] for entry in head_results], axis=1)
    grad_query = jnp.concatenate([entry[1] for entry in head_results], axis=1)
    grad_key = jnp.concatenate([entry[2] for entry in head_results], axis=1)
    grad_value = jnp.concatenate([entry[3] for entry in head_results], axis=1)
    attended = jnp.dot(mixed_heads, w_out, preferred_element_type=jnp.float32).astype(jnp.bfloat16)
    grad_stack = jnp.stack([contract(normed, grad_query, 0, 0), contract(normed, grad_key, 0, 0), contract(normed, grad_value, 0, 0), contract(mixed_heads, upstream, 0, 0)])
    return (attended, grad_stack)

def reference(signal, fir_taps, neighbours, live_mask, lap_coef, w_query, w_key, w_value, w_out, cotangent):
    rim_width = TAPS - 1
    filter_table = toeplitz(fir_taps).astype(jnp.float32)
    alive_f = live_mask.astype(jnp.float32)
    nbr_alive = jnp.take(alive_f, neighbours)

    def section_one(one_row):
        extended = jnp.concatenate([jnp.zeros((CONTACTS, rim_width), jnp.bfloat16), one_row], axis=1).astype(jnp.float32)
        blocks = extended.reshape(CONTACTS, SAMPLES // rim_width + 1, rim_width)
        windows = jnp.concatenate([blocks[:, :-1], blocks[:, 1:]], axis=2)
        filtered = jnp.einsum('cjw,cwu->cju', windows, filter_table, precision=lax.Precision.HIGHEST)
        filtered = filtered.reshape(CONTACTS, SAMPLES).astype(jnp.bfloat16)
        return laplace(filtered, filtered, neighbours, nbr_alive, alive_f, lap_coef)
    ready = lax.map(section_one, signal)

    def to_groups(whole):
        return whole.reshape(BATCH, CONTACTS, PATCHES, PATCH).transpose(0, 2, 1, 3).reshape(BATCH * PATCHES, CONTACTS, PATCH)

    def run_group(running, inputs_pair):
        attended, grad_stack = group_step(inputs_pair[0], inputs_pair[1], alive_f, w_query, w_key, w_value, w_out)
        return (running + grad_stack, attended)
    running, attended = lax.scan(run_group, jnp.zeros((4, PATCH, PATCH), jnp.float32), (to_groups(ready), to_groups(cotangent)))
    attended = attended.reshape(BATCH, PATCHES, CONTACTS, PATCH).transpose(0, 2, 1, 3).reshape(BATCH, CONTACTS, SAMPLES)
    return (attended, running * (BATCH * PATCHES * CONTACTS) ** (-0.5))
```

```python
import functools

import jax
import jax.numpy as jnp
from jax import lax
from jax.experimental import pallas as pl
from jax.experimental.pallas import tpu as pltpu
from jax.sharding import PartitionSpec as P

HEADS = 4
CORES = 2
HALVES = 2
SIDE_LAYERS = 4
MESH = pl.DeviceIdType.MESH
F32 = jnp.float32
BF16 = jnp.bfloat16


def nn(left, right):
    return lax.dot_general(left, right, (((1,), (0,)), ((), ())), preferred_element_type=F32)


def nt(left, right):
    return lax.dot_general(left, right, (((1,), (1,)), ((), ())), preferred_element_type=F32)


def build_tables(taps_ref, table_ref):
    contacts, taps = taps_ref.shape
    width = taps - 1
    values = taps_ref[...].astype(F32)
    source = lax.broadcasted_iota(jnp.int32, (width, width), 0)
    target = lax.broadcasted_iota(jnp.int32, (width, width), 1)
    for c in range(contacts):
        row = jnp.broadcast_to(values[c : c + 1, :width], (width, width))
        turned = pltpu.roll(row, 0, 1, stride=1, stride_axis=0)
        last = jnp.broadcast_to(values[c : c + 1, width:], (width, width))
        own = jnp.where(target >= source, turned, 0.0)
        before = jnp.where(target < source, turned, jnp.where(target == source, last, 0.0))
        table_ref[c, :, :width] = before.astype(BF16)
        table_ref[c, :, width:] = own.astype(BF16)


def spread_blocks(signal_ref, rows_ref, width):
    batch, contacts, length = signal_ref.shape
    blocks = length // width
    for b in range(batch):
        for j in range(blocks):
            at = (b * blocks + j) * contacts
            rows_ref[at : at + contacts, :] = signal_ref[
                b, :, j * width : (j + 1) * width
            ].astype(F32)


def run_filter(rows_ref, table_ref, before_ref, own_ref, filtered_ref):
    batch, contacts, length = filtered_ref.shape
    width = table_ref.shape[1]
    blocks = length // width
    count = batch * blocks
    for c in range(contacts):
        picked = rows_ref[pl.ds(c, count, stride=contacts), :].astype(BF16)
        both = nn(picked, table_ref[c])
        before_ref[pl.ds(c, count, stride=contacts), :] = both[:, :width]
        own_ref[pl.ds(c, count, stride=contacts), :] = both[:, width:]
    for b in range(batch):
        for j in range(1, blocks):
            at = (b * blocks + j) * contacts
            filtered_ref[b, :, j * width : (j + 1) * width] = (
                before_ref[at - contacts : at, :] + own_ref[at : at + contacts, :]
            ).astype(BF16)


def finish_filter(halo_ref, rows_ref, table_ref, before_ref, own_ref, filtered_ref):
    batch, contacts, length = filtered_ref.shape
    width = table_ref.shape[1]
    blocks = length // width
    for b in range(batch):
        rows_ref[b * contacts : (b + 1) * contacts, :] = halo_ref[b].astype(F32)
    for c in range(contacts):
        picked = rows_ref[pl.ds(c, batch, stride=contacts), :].astype(BF16)
        before_ref[pl.ds(c, batch, stride=contacts), :] = nn(picked, table_ref[c, :, :width])
    for b in range(batch):
        at = b * blocks * contacts
        filtered_ref[b, :, :width] = (
            before_ref[b * contacts : (b + 1) * contacts, :] + own_ref[at : at + contacts, :]
        ).astype(BF16)


def count_hits(neighbours_ref, alive_ref, coef_ref, hits_ref, columns_ref):
    slots, tokens = neighbours_ref.shape
    alive_row = alive_ref[...].astype(F32)
    stacked = jnp.concatenate(
        [neighbours_ref[...].astype(F32), alive_row, coef_ref[...]]
        + [jnp.zeros((8 - slots - 2, tokens), F32)],
        axis=0,
    )
    columns = stacked.T
    step = 128
    for at in range(0, tokens, step):
        ids = lax.broadcasted_iota(jnp.int32, (step, tokens), 1).astype(F32)
        hits = jnp.zeros((step, tokens), F32)
        for k in range(slots):
            hits = hits + jnp.where(columns[at : at + step, k : k + 1] == ids, alive_row, 0.0)
        hits_ref[at : at + step, :] = hits.astype(BF16)
        total = jnp.sum(hits, axis=1, keepdims=True)
        columns_ref[0, at : at + step, :] = jnp.broadcast_to(total, (step, 128))
    alive = columns[:, slots : slots + 1]
    columns_ref[1] = jnp.broadcast_to(alive, (tokens, 128))
    columns_ref[2] = jnp.broadcast_to(columns[:, slots + 1 : slots + 2], (tokens, 128))
    columns_ref[3] = jnp.broadcast_to(jnp.where(alive > 0, 0.0, -1e30), (tokens, 128))


def wide(column, lanes):
    return jnp.concatenate([column] * (lanes // column.shape[1]), axis=1)


def project_tokens(tokens_ref, hits_ref, columns_ref, weights, work):
    w_query_ref, w_key_ref, w_value_ref, _ = weights
    tokens, patch = tokens_ref.shape
    middle = tokens_ref[...]
    beside = nn(hits_ref[...], middle)
    middle = middle.astype(F32)
    alive_count, alive, coef = [wide(columns_ref[k], patch) for k in range(3)]
    ready = (alive * (middle + coef * (beside - alive_count * middle))).astype(BF16).astype(F32)
    mean = jnp.sum(ready * ready, axis=1, keepdims=True) * (1.0 / patch)
    normed_f = ready * lax.rsqrt(mean + 1e-05)
    normed = normed_f.astype(BF16)
    work["normed_t"][...] = normed_f.T.astype(BF16)
    score_scale = (patch // HEADS) ** (-0.5)
    query = nn(normed, w_query_ref[...]).astype(BF16).astype(F32)
    work["query"][...] = (query * score_scale).astype(BF16)
    keys = nn(normed, w_key_ref[...]).astype(BF16)
    work["key"][...] = keys
    work["key_t"][...] = keys.astype(F32).T.astype(BF16)
    values = nn(normed, w_value_ref[...]).astype(BF16)
    work["value"][...] = values
    work["value_t"][...] = values.astype(F32).T.astype(BF16)


def attend(upstream_ref, columns_ref, weights, work):
    w_out_ref = weights[3]
    tokens, patch = upstream_ref.shape
    head = patch // HEADS
    score_scale = head ** (-0.5)
    back = nt(upstream_ref[...], w_out_ref[...]).astype(BF16)
    work["back"][...] = back
    work["back_t"][...] = back.astype(F32).T
    pair = 2 * head
    lane = lax.broadcasted_iota(jnp.int32, (tokens, pair), 1)
    bias = wide(columns_ref[3], tokens)
    for p in range(HEADS // 2):
        at = slice(p * pair, (p + 1) * pair)
        grad_key = None
        grad_value = None
        for s in range(2):
            h = 2 * p + s
            rows = slice(h * head, (h + 1) * head)
            inside = (lane >= s * head) & (lane < (s + 1) * head)
            query = jnp.where(inside, work["query"][:, at].astype(F32), 0.0).astype(BF16)
            backward = jnp.where(inside, work["back"][:, at].astype(F32), 0.0).astype(BF16)
            scores = nt(work["key"][:, at], query) + bias
            raised = jnp.exp(scores - jnp.max(scores, axis=0, keepdims=True))
            prob = raised * (1.0 / jnp.sum(raised, axis=0, keepdims=True))
            prob_low = prob.astype(BF16)
            mixed_t = nn(work["value_t"][rows, :], prob_low).astype(BF16)
            work["mixed_t"][rows, :] = mixed_t
            inner = jnp.sum(
                work["back_t"][rows, :] * mixed_t.astype(F32), axis=0, keepdims=True
            )
            grad_prob = nt(work["value"][:, at], backward)
            grad_score = (prob * (grad_prob - inner)).astype(BF16)
            part_value = nn(prob_low, backward)
            part_key = nn(grad_score, query)
            grad_value = part_value if s == 0 else grad_value + part_value
            grad_key = part_key if s == 0 else grad_key + part_key
            work["grad_query_t"][rows, :] = (
                nn(work["key_t"][rows, :], grad_score) * score_scale
            ).astype(BF16)
        work["grad_key"][:, at] = grad_key.astype(BF16)
        work["grad_value"][:, at] = grad_value.astype(BF16)


def weight_grads(grads_ref, upstream_ref, work, grad_scale):
    patch = upstream_ref.shape[1]
    normed_t = work["normed_t"][...]
    products = (
        nt(normed_t, work["grad_query_t"][...]),
        nn(normed_t, work["grad_key"][...]),
        nn(normed_t, work["grad_value"][...]),
        nn(work["mixed_t"][...], upstream_ref[...]),
    )
    for k, product in enumerate(products):
        grads_ref[k * patch : (k + 1) * patch, :] = product * grad_scale


WORK = (
    ("query", 0, BF16),
    ("key", 0, BF16),
    ("value", 0, BF16),
    ("back", 0, BF16),
    ("grad_key", 0, BF16),
    ("grad_value", 0, BF16),
    ("key_t", 1, BF16),
    ("value_t", 1, BF16),
    ("back_t", 1, F32),
    ("normed_t", 1, BF16),
    ("mixed_t", 1, BF16),
    ("grad_query_t", 1, BF16),
)


def step_kernel(
    slabs,
    members,
    grad_scale,
    signal_ref,
    taps_ref,
    neighbours_ref,
    alive_ref,
    coef_ref,
    w_query_ref,
    w_key_ref,
    w_value_ref,
    w_out_ref,
    cotangent_ref,
    returned_ref,
    summed_ref,
    halo_ref,
    table_ref,
    rows_ref,
    before_ref,
    own_ref,
    filtered_ref,
    tokens_ref,
    upstream_ref,
    attended_ref,
    hits_ref,
    columns_ref,
    grads_ref,
    core_out,
    core_in,
    plane_sum,
    plane_out,
    plane_in,
    depth_in,
    result,
    send_sem,
    recv_sem,
    local_sem,
    *work_refs,
):
    work = {entry[0]: ref for entry, ref in zip(WORK, work_refs)}
    weights = (w_query_ref, w_key_ref, w_value_ref, w_out_ref)
    slab = lax.axis_index("tm")
    me = lax.axis_index("contact")
    core = lax.rem(slab, CORES)
    side = lax.rem(slab // CORES, HALVES)
    column = slab // (CORES * HALVES)
    columns = slabs // (CORES * HALVES)
    layers = SIDE_LAYERS
    lines = members // layers
    layer = me // lines
    line = lax.rem(me, lines)
    plane = columns * lines
    depth = HALVES * layers
    spot = column * lines + line
    level = side * layers + layer

    batch, contacts, length = signal_ref.shape
    width = taps_ref.shape[1] - 1
    tokens, patch = tokens_ref.shape
    per_row = length // patch
    total = grads_ref.shape[0]
    half = total // CORES
    piece = half // plane
    has_next = slab < slabs - 1
    has_prior = slab > 0

    def slab_at(column_at, side_at, core_at):
        return (column_at * HALVES + side_at) * CORES + core_at

    core_peer = (slab_at(column, side, 1 - core), me)

    def plane_peer(step):
        at = lax.rem(spot + step, plane)
        return at, (slab_at(at // lines, side, core), layer * lines + lax.rem(at, lines))

    def depth_peer(step):
        at = lax.rem(level + step, depth)
        return slab_at(column, at // layers, core), lax.rem(at, layers) * lines + line

    def contact_peer(step):
        return slab, lax.rem(me + step, members)

    barrier = pltpu.get_barrier_semaphore()

    def greet(device):
        pl.semaphore_signal(barrier, inc=1, device_id=device, device_id_type=MESH)

    def greet_contact(step, carry):
        greet(contact_peer(step))
        return carry

    def greet_plane(step, carry):
        greet(plane_peer(step)[1])
        return carry

    def greet_depth(step, carry):
        greet(depth_peer(step))
        return carry

    lax.fori_loop(1, members, greet_contact, 0)

    @pl.when(has_next)
    def _():
        greet((slab + 1, me))

    @pl.when(has_prior)
    def _():
        greet((slab - 1, me))

    lax.fori_loop(1, plane, greet_plane, 0)
    lax.fori_loop(1, depth, greet_depth, 0)
    greet(core_peer)

    build_tables(taps_ref, table_ref)
    spread_blocks(signal_ref, rows_ref, width)
    run_filter(rows_ref, table_ref, before_ref, own_ref, filtered_ref)

    greetings = members + plane + depth - 2 + has_next.astype(jnp.int32)
    pl.semaphore_wait(barrier, greetings + has_prior.astype(jnp.int32))

    def remote(source, target, which, device):
        return pltpu.make_async_remote_copy(
            src_ref=source,
            dst_ref=target,
            send_sem=send_sem.at[which],
            recv_sem=recv_sem.at[which],
            device_id=device,
            device_id_type=MESH,
        )

    halo = remote(
        signal_ref.at[:, :, pl.ds(length - width, width)],
        halo_ref,
        0,
        (lax.rem(slab + 1, slabs), me),
    )

    @pl.when(has_next)
    def _():
        halo.start()

    def block_of(ref, group):
        return ref.at[
            group // per_row, :, pl.ds(pl.multiple_of(lax.rem(group, per_row) * patch, patch), patch)
        ]

    def rows_of(ref, member):
        return ref.at[pl.ds(pl.multiple_of(member * contacts, contacts), contacts)]

    def send_tokens(peer):
        remote(
            block_of(filtered_ref, peer), rows_of(tokens_ref, me), 2, (slab, peer)
        ).start()

    def send_ready(step, carry):
        peer = lax.rem(me + step, members)

        @pl.when(lax.rem(peer, per_row) != 0)
        def _():
            send_tokens(peer)

        return carry

    def send_upstream(step, carry):
        peer = lax.rem(me + step, members)
        remote(
            block_of(cotangent_ref, peer), rows_of(upstream_ref, me), 1, (slab, peer)
        ).start()
        return carry

    lax.fori_loop(1, members, send_ready, 0)
    lax.fori_loop(1, members, send_upstream, 0)
    own_upstream = pltpu.make_async_copy(
        block_of(cotangent_ref, me), rows_of(upstream_ref, me), local_sem.at[0]
    )
    own_upstream.start()

    @pl.when(has_prior)
    def _():
        halo.wait_recv()

    @pl.when(jnp.logical_not(has_prior))
    def _():
        halo_ref[...] = jnp.zeros_like(halo_ref)

    finish_filter(halo_ref, rows_ref, table_ref, before_ref, own_ref, filtered_ref)

    def send_first(step, carry):
        peer = lax.rem(me // per_row + step, batch) * per_row

        @pl.when(peer != me)
        def _():
            send_tokens(peer)

        return carry

    lax.fori_loop(0, batch, send_first, 0)
    own_tokens = pltpu.make_async_copy(
        block_of(filtered_ref, me), rows_of(tokens_ref, me), local_sem.at[1]
    )
    own_tokens.start()
    count_hits(neighbours_ref, alive_ref, coef_ref, hits_ref, columns_ref)

    def all_but_one(ref, which):
        rest = ref.at[pl.ds(0, (members - 1) * contacts)]
        return remote(rest, rest, which, core_peer)

    tokens_copy = all_but_one(tokens_ref, 2)
    upstream_copy = all_but_one(upstream_ref, 1)
    own_tokens.wait()
    tokens_copy.wait_recv()
    project_tokens(tokens_ref, hits_ref, columns_ref, weights, work)
    own_upstream.wait()
    upstream_copy.wait_recv()
    attend(upstream_ref, columns_ref, weights, work)
    weight_grads(grads_ref, upstream_ref, work, grad_scale)

    other_half = pl.ds(pl.multiple_of((1 - core) * half, half), half)
    my_half = pl.ds(pl.multiple_of(core * half, half), half)
    core_out[...] = grads_ref[other_half, :].astype(BF16)
    core_copy = remote(core_out, core_in, 3, core_peer)
    core_copy.start()

    mixed = work["mixed_t"][...].astype(F32).T.astype(BF16)
    attended_ref[...] = nn(mixed, w_out_ref[...]).astype(BF16)

    core_copy.wait_recv()
    plane_sum[...] = grads_ref[my_half, :] + core_in[...].astype(F32)
    plane_out[...] = plane_sum[...].astype(BF16)

    def piece_of(ref, first, at):
        return ref.at[pl.ds(pl.multiple_of(first + at * piece, piece), piece)]

    def scatter(step, carry):
        at, device = plane_peer(step)
        remote(piece_of(plane_out, 0, at), plane_in.at[step - 1], 4, device).start()
        return carry

    lax.fori_loop(1, plane, scatter, 0)

    def give_back(step, carry):
        peer = lax.rem(me + step, members)
        remote(
            rows_of(attended_ref, peer), block_of(returned_ref, me), 5, (slab, peer)
        ).start()
        return carry

    lax.fori_loop(1, members, give_back, 0)
    own_back = pltpu.make_async_copy(
        rows_of(attended_ref, me), block_of(returned_ref, me), local_sem.at[0]
    )
    own_back.start()

    scatter_copy = remote(plane_in, plane_in, 4, core_peer)
    scatter_copy.wait_recv()
    running = piece_of(plane_sum, 0, spot)[...]
    for step in range(1, plane):
        running = running + plane_in[step - 1].astype(F32)
    depth_in[level] = running.astype(BF16)

    def exchange(step, carry):
        remote(depth_in.at[level], depth_in.at[level], 6, depth_peer(step)).start()
        return carry

    lax.fori_loop(1, depth, exchange, 0)
    rest = depth_in.at[pl.ds(0, depth - 1)]
    depth_copy = remote(rest, rest, 6, core_peer)
    depth_copy.wait_recv()
    running = depth_in[0].astype(F32)
    for at in range(1, depth):
        running = running + depth_in[at].astype(F32)
    own_piece = piece_of(result, core * half, spot)
    own_piece[...] = running.astype(BF16)

    def gather(step, carry):
        remote(own_piece, own_piece, 7, plane_peer(step)[1]).start()
        return carry

    lax.fori_loop(1, plane, gather, 0)
    rest = result.at[pl.ds(0, (plane - 1) * piece)]
    gather_copy = remote(rest, rest, 7, core_peer)
    gather_copy.wait_recv()

    own_half = result.at[my_half]
    last_copy = remote(own_half, own_half, 8, core_peer)
    last_copy.start()
    last_copy.wait_recv()
    summed = pltpu.make_async_copy(result, summed_ref, local_sem.at[1])
    summed.start()

    @pl.when(has_next)
    def _():
        halo.wait_send()

    tokens_copy.wait_send()
    upstream_copy.wait_send()
    core_copy.wait_send()
    scatter_copy.wait_send()
    depth_copy.wait_send()
    gather_copy.wait_send()
    last_copy.wait_send()
    own_back.wait()
    back_copy = all_but_one(attended_ref, 5)
    back_copy.wait_recv()
    back_copy.wait_send()
    summed.wait()


def finish_kernel(returned_ref, summed_ref, out_ref, grads_ref, held, wide_ref, sems):
    parts = held.shape[0]
    rows = held.shape[1]
    back = pltpu.make_async_copy(returned_ref, out_ref, sems.at[0])
    back.start()
    loads = [
        pltpu.make_async_copy(
            summed_ref.at[pl.ds(k * rows, rows)], held.at[k], sems.at[1 + k]
        )
        for k in range(parts)
    ]
    stores = [
        pltpu.make_async_copy(wide_ref.at[k], grads_ref.at[k], sems.at[1 + parts + k])
        for k in range(parts)
    ]
    for load in loads:
        load.start()
    for k in range(parts):
        loads[k].wait()
        wide_ref[k] = held[k].astype(F32)
        stores[k].start()
    for store in stores:
        store.wait()
    back.wait()


VMEM = pl.BlockSpec(memory_space=pltpu.VMEM)
ANY = pl.BlockSpec(memory_space=pl.ANY)


def local(
    signal, fir_taps, neighbours, live_mask, lap_coef, w_query, w_key, w_value, w_out, cotangent
):
    batch, contacts, length = signal.shape
    width = fir_taps.shape[1] - 1
    patch = w_query.shape[0]
    slabs = lax.axis_size("tm")
    members = lax.axis_size("contact")
    tokens = neighbours.shape[0]
    blocks = length // width
    groups = batch * (length // patch) * slabs
    plane = slabs // (CORES * HALVES) * (members // SIDE_LAYERS)
    depth = HALVES * SIDE_LAYERS
    total = 4 * patch
    half = total // CORES
    piece = half // plane
    padded = batch * blocks * contacts
    work = [
        pltpu.VMEM((patch, tokens) if turned else (tokens, patch), dtype)
        for _, turned, dtype in WORK
    ]
    returned, summed = pl.pallas_call(
        functools.partial(step_kernel, slabs, members, (groups * tokens) ** (-0.5)),
        out_shape=(
            jax.ShapeDtypeStruct(signal.shape, BF16),
            jax.ShapeDtypeStruct((total, patch), BF16),
        ),
        in_specs=[VMEM] * 9 + [ANY],
        out_specs=(ANY, ANY),
        scratch_shapes=[
            pltpu.VMEM((batch, contacts, width), BF16),
            pltpu.VMEM((contacts, width, 2 * width), BF16),
            pltpu.VMEM((padded, width), F32),
            pltpu.VMEM((padded, width), F32),
            pltpu.VMEM((padded, width), F32),
            pltpu.VMEM((batch, contacts, length), BF16),
            pltpu.VMEM((tokens, patch), BF16),
            pltpu.VMEM((tokens, patch), BF16),
            pltpu.VMEM((tokens, patch), BF16),
            pltpu.VMEM((tokens, tokens), BF16),
            pltpu.VMEM((4, tokens, 128), F32),
            pltpu.VMEM((total, patch), F32),
            pltpu.VMEM((half, patch), BF16),
            pltpu.VMEM((half, patch), BF16),
            pltpu.VMEM((half, patch), F32),
            pltpu.VMEM((half, patch), BF16),
            pltpu.VMEM((plane - 1, piece, patch), BF16),
            pltpu.VMEM((depth, piece, patch), BF16),
            pltpu.VMEM((total, patch), BF16),
            pltpu.SemaphoreType.DMA((9,)),
            pltpu.SemaphoreType.DMA((9,)),
            pltpu.SemaphoreType.DMA((2,)),
        ]
        + work,
        compiler_params=pltpu.CompilerParams(collective_id=0, has_side_effects=True),
    )(
        signal,
        fir_taps,
        neighbours.T,
        live_mask.reshape(1, tokens),
        lap_coef.reshape(1, tokens),
        w_query,
        w_key,
        w_value,
        w_out,
        cotangent,
    )
    return pl.pallas_call(
        finish_kernel,
        out_shape=(
            jax.ShapeDtypeStruct(signal.shape, BF16),
            jax.ShapeDtypeStruct((4, patch, patch), F32),
        ),
        in_specs=[ANY, ANY],
        out_specs=(ANY, ANY),
        scratch_shapes=[
            pltpu.VMEM((4, patch, patch), BF16),
            pltpu.VMEM((4, patch, patch), F32),
            pltpu.SemaphoreType.DMA((9,)),
        ],
    )(returned, summed)


def solution(mesh):
    in_specs = (
        P(None, "contact", "tm"),
        P("contact", None),
        P(),
        P(),
        P(),
        P(),
        P(),
        P(),
        P(),
        P(None, "contact", "tm"),
    )
    out_specs = (P(None, "contact", "tm"), P())
    return jax.shard_map(local, mesh=mesh, in_specs=in_specs, out_specs=out_specs, check_vma=False)
```

```python
import functools

import jax
import jax.numpy as jnp
from jax import lax
from jax.experimental import pallas as pl
from jax.experimental.pallas import tpu as pltpu
from jax.sharding import PartitionSpec as P

HEADS = 4
CORES = 2
HALVES = 2
SIDE_LAYERS = 4
VMEM_BYTES = 32 * 2**20
MESH = pl.DeviceIdType.MESH
F32 = jnp.float32
BF16 = jnp.bfloat16


def nn(left, right):
    return lax.dot_general(left, right, (((1,), (0,)), ((), ())), preferred_element_type=F32)


def nt(left, right):
    return lax.dot_general(left, right, (((1,), (1,)), ((), ())), preferred_element_type=F32)


def build_tables(taps_ref, table_ref):
    contacts, taps = taps_ref.shape
    width = taps - 1
    values = taps_ref[...].astype(F32)
    source = lax.broadcasted_iota(jnp.int32, (width, width), 0)
    target = lax.broadcasted_iota(jnp.int32, (width, width), 1)
    for c in range(contacts):
        row = jnp.broadcast_to(values[c : c + 1, :width], (width, width))
        turned = pltpu.roll(row, 0, 1, stride=1, stride_axis=0)
        last = jnp.broadcast_to(values[c : c + 1, width:], (width, width))
        own = jnp.where(target >= source, turned, 0.0)
        before = jnp.where(target < source, turned, jnp.where(target == source, last, 0.0))
        table_ref[c, :, :width] = before.astype(BF16)
        table_ref[c, :, width:] = own.astype(BF16)


def spread_blocks(signal_ref, rows_ref, width):
    batch, contacts, length = signal_ref.shape
    blocks = length // width
    for b in range(batch):
        for j in range(blocks):
            at = (b * blocks + j) * contacts
            rows_ref[at : at + contacts, :] = signal_ref[
                b, :, j * width : (j + 1) * width
            ].astype(F32)


def run_filter(rows_ref, table_ref, before_ref, own_ref, filtered_ref):
    batch, contacts, length = filtered_ref.shape
    width = table_ref.shape[1]
    blocks = length // width
    count = batch * blocks
    for c in range(contacts):
        picked = rows_ref[pl.ds(c, count, stride=contacts), :].astype(BF16)
        both = nn(picked, table_ref[c])
        before_ref[pl.ds(c, count, stride=contacts), :] = both[:, :width]
        own_ref[pl.ds(c, count, stride=contacts), :] = both[:, width:]
    for b in range(batch):
        for j in range(1, blocks):
            at = (b * blocks + j) * contacts
            filtered_ref[b, :, j * width : (j + 1) * width] = (
                before_ref[at - contacts : at, :] + own_ref[at : at + contacts, :]
            ).astype(BF16)


def finish_filter(halo_ref, rows_ref, table_ref, before_ref, own_ref, filtered_ref):
    batch, contacts, length = filtered_ref.shape
    width = table_ref.shape[1]
    blocks = length // width
    for b in range(batch):
        rows_ref[b * contacts : (b + 1) * contacts, :] = halo_ref[b].astype(F32)
    for c in range(contacts):
        picked = rows_ref[pl.ds(c, batch, stride=contacts), :].astype(BF16)
        before_ref[pl.ds(c, batch, stride=contacts), :] = nn(picked, table_ref[c, :, :width])
    for b in range(batch):
        at = b * blocks * contacts
        filtered_ref[b, :, :width] = (
            before_ref[b * contacts : (b + 1) * contacts, :] + own_ref[at : at + contacts, :]
        ).astype(BF16)


def count_hits(neighbours_ref, alive_ref, coef_ref, hits_ref, columns_ref):
    slots, tokens = neighbours_ref.shape
    alive_row = alive_ref[...].astype(F32)
    stacked = jnp.concatenate(
        [neighbours_ref[...].astype(F32), alive_row, coef_ref[...]]
        + [jnp.zeros((8 - slots - 2, tokens), F32)],
        axis=0,
    )
    columns = stacked.T
    step = 128
    for at in range(0, tokens, step):
        ids = lax.broadcasted_iota(jnp.int32, (step, tokens), 1).astype(F32)
        hits = jnp.zeros((step, tokens), F32)
        for k in range(slots):
            hits = hits + jnp.where(columns[at : at + step, k : k + 1] == ids, alive_row, 0.0)
        hits_ref[at : at + step, :] = hits.astype(BF16)
        total = jnp.sum(hits, axis=1, keepdims=True)
        columns_ref[0, at : at + step, :] = jnp.broadcast_to(total, (step, 128))
    alive = columns[:, slots : slots + 1]
    columns_ref[1] = jnp.broadcast_to(alive, (tokens, 128))
    columns_ref[2] = jnp.broadcast_to(columns[:, slots + 1 : slots + 2], (tokens, 128))
    columns_ref[3] = jnp.broadcast_to(jnp.where(alive > 0, 0.0, -1e30), (tokens, 128))


def wide(column, lanes):
    return jnp.concatenate([column] * (lanes // column.shape[1]), axis=1)


def project_tokens(tokens_ref, hits_ref, columns_ref, weights, work):
    w_query_ref, w_key_ref, w_value_ref, _ = weights
    tokens, patch = tokens_ref.shape
    middle = tokens_ref[...]
    beside = nn(hits_ref[...], middle)
    middle = middle.astype(F32)
    alive_count, alive, coef = [wide(columns_ref[k], patch) for k in range(3)]
    ready = (alive * (middle + coef * (beside - alive_count * middle))).astype(BF16).astype(F32)
    mean = jnp.sum(ready * ready, axis=1, keepdims=True) * (1.0 / patch)
    normed_f = ready * lax.rsqrt(mean + 1e-05)
    normed = normed_f.astype(BF16)
    work["normed_t"][...] = normed_f.T.astype(BF16)
    score_scale = (patch // HEADS) ** (-0.5)
    query = nn(normed, w_query_ref[...]).astype(BF16).astype(F32)
    work["query"][...] = (query * score_scale).astype(BF16)
    keys = nn(normed, w_key_ref[...]).astype(BF16)
    work["key"][...] = keys
    work["key_t"][...] = keys.astype(F32).T.astype(BF16)
    values = nn(normed, w_value_ref[...]).astype(BF16)
    work["value"][...] = values
    work["value_t"][...] = values.astype(F32).T.astype(BF16)


def attend(upstream_ref, columns_ref, weights, work):
    w_out_ref = weights[3]
    tokens, patch = upstream_ref.shape
    head = patch // HEADS
    score_scale = head ** (-0.5)
    back = nt(upstream_ref[...], w_out_ref[...]).astype(BF16)
    work["back"][...] = back
    work["back_t"][...] = back.astype(F32).T
    pair = 2 * head
    lane = lax.broadcasted_iota(jnp.int32, (tokens, pair), 1)
    bias = wide(columns_ref[3], tokens)
    for p in range(HEADS // 2):
        at = slice(p * pair, (p + 1) * pair)
        grad_key = None
        grad_value = None
        for s in range(2):
            h = 2 * p + s
            rows = slice(h * head, (h + 1) * head)
            inside = (lane >= s * head) & (lane < (s + 1) * head)
            query = jnp.where(inside, work["query"][:, at].astype(F32), 0.0).astype(BF16)
            backward = jnp.where(inside, work["back"][:, at].astype(F32), 0.0).astype(BF16)
            scores = nt(work["key"][:, at], query) + bias
            raised = jnp.exp(scores - jnp.max(scores, axis=0, keepdims=True))
            prob = raised * (1.0 / jnp.sum(raised, axis=0, keepdims=True))
            prob_low = prob.astype(BF16)
            mixed_t = nn(work["value_t"][rows, :], prob_low).astype(BF16)
            work["mixed_t"][rows, :] = mixed_t
            inner = jnp.sum(
                work["back_t"][rows, :] * mixed_t.astype(F32), axis=0, keepdims=True
            )
            grad_prob = nt(work["value"][:, at], backward)
            grad_score = (prob * (grad_prob - inner)).astype(BF16)
            part_value = nn(prob_low, backward)
            part_key = nn(grad_score, query)
            grad_value = part_value if s == 0 else grad_value + part_value
            grad_key = part_key if s == 0 else grad_key + part_key
            work["grad_query_t"][rows, :] = (
                nn(work["key_t"][rows, :], grad_score) * score_scale
            ).astype(BF16)
        work["grad_key"][:, at] = grad_key.astype(BF16)
        work["grad_value"][:, at] = grad_value.astype(BF16)


def weight_grads(grads_ref, upstream_ref, work, grad_scale):
    patch = upstream_ref.shape[1]
    normed_t = work["normed_t"][...]
    products = (
        nt(normed_t, work["grad_query_t"][...]),
        nn(normed_t, work["grad_key"][...]),
        nn(normed_t, work["grad_value"][...]),
        nn(work["mixed_t"][...], upstream_ref[...]),
    )
    for k, product in enumerate(products):
        grads_ref[k * patch : (k + 1) * patch, :] = product * grad_scale


WORK = (
    ("query", 0, BF16),
    ("key", 0, BF16),
    ("value", 0, BF16),
    ("back", 0, BF16),
    ("grad_key", 0, BF16),
    ("grad_value", 0, BF16),
    ("key_t", 1, BF16),
    ("value_t", 1, BF16),
    ("back_t", 1, F32),
    ("normed_t", 1, BF16),
    ("mixed_t", 1, BF16),
    ("grad_query_t", 1, BF16),
)


def step_kernel(
    slabs,
    members,
    grad_scale,
    signal_hbm,
    taps_hbm,
    neighbours_hbm,
    alive_hbm,
    coef_hbm,
    w_query_hbm,
    w_key_hbm,
    w_value_hbm,
    w_out_hbm,
    cotangent_ref,
    returned_ref,
    summed_ref,
    signal_ref,
    taps_ref,
    neighbours_ref,
    alive_ref,
    coef_ref,
    w_query_ref,
    w_key_ref,
    w_value_ref,
    w_out_ref,
    halo_ref,
    table_ref,
    rows_ref,
    before_ref,
    own_ref,
    filtered_ref,
    tokens_ref,
    upstream_ref,
    attended_ref,
    hits_ref,
    columns_ref,
    grads_ref,
    core_out,
    core_in,
    plane_sum,
    plane_out,
    plane_in,
    depth_in,
    result,
    send_sem,
    recv_sem,
    local_sem,
    load_sem,
    *work_refs,
):
    loads = [
        pltpu.make_async_copy(source, target, load_sem.at[k])
        for k, (source, target) in enumerate(
            (
                (signal_hbm, signal_ref),
                (taps_hbm, taps_ref),
                (neighbours_hbm, neighbours_ref),
                (alive_hbm, alive_ref),
                (coef_hbm, coef_ref),
                (w_query_hbm, w_query_ref),
                (w_key_hbm, w_key_ref),
                (w_value_hbm, w_value_ref),
                (w_out_hbm, w_out_ref),
            )
        )
    ]
    for load in loads:
        load.start()
    work = {entry[0]: ref for entry, ref in zip(WORK, work_refs)}
    weights = (w_query_ref, w_key_ref, w_value_ref, w_out_ref)
    slab = lax.axis_index("tm")
    me = lax.axis_index("contact")
    core = lax.rem(slab, CORES)
    side = lax.rem(slab // CORES, HALVES)
    column = slab // (CORES * HALVES)
    columns = slabs // (CORES * HALVES)
    layers = SIDE_LAYERS
    lines = members // layers
    layer = me // lines
    line = lax.rem(me, lines)
    plane = columns * lines
    depth = HALVES * layers
    spot = column * lines + line
    level = side * layers + layer

    batch, contacts, length = signal_ref.shape
    width = taps_ref.shape[1] - 1
    tokens, patch = tokens_ref.shape
    per_row = length // patch
    total = grads_ref.shape[0]
    half = total // CORES
    piece = half // plane
    has_next = slab < slabs - 1
    has_prior = slab > 0

    def slab_at(column_at, side_at, core_at):
        return (column_at * HALVES + side_at) * CORES + core_at

    core_peer = (slab_at(column, side, 1 - core), me)

    def plane_peer(step):
        at = lax.rem(spot + step, plane)
        return at, (slab_at(at // lines, side, core), layer * lines + lax.rem(at, lines))

    def depth_peer(step):
        at = lax.rem(level + step, depth)
        return slab_at(column, at // layers, core), lax.rem(at, layers) * lines + line

    def contact_peer(step):
        return slab, lax.rem(me + step, members)

    barrier = pltpu.get_barrier_semaphore()

    def greet(device):
        pl.semaphore_signal(barrier, inc=1, device_id=device, device_id_type=MESH)

    def greet_contact(step, carry):
        greet(contact_peer(step))
        return carry

    def greet_plane(step, carry):
        greet(plane_peer(step)[1])
        return carry

    def greet_depth(step, carry):
        greet(depth_peer(step))
        return carry

    @pl.when(has_next)
    def _():
        greet((slab + 1, me))

    @pl.when(has_prior)
    def _():
        greet((slab - 1, me))

    lax.fori_loop(1, members, greet_contact, 0)
    lax.fori_loop(1, plane, greet_plane, 0)
    lax.fori_loop(1, depth, greet_depth, 0)
    greet(core_peer)

    for load in loads:
        load.wait()
    build_tables(taps_ref, table_ref)
    spread_blocks(signal_ref, rows_ref, width)
    run_filter(rows_ref, table_ref, before_ref, own_ref, filtered_ref)

    greetings = members + plane + depth - 2 + has_next.astype(jnp.int32)
    pl.semaphore_wait(barrier, greetings + has_prior.astype(jnp.int32))

    def remote(source, target, which, device):
        return pltpu.make_async_remote_copy(
            src_ref=source,
            dst_ref=target,
            send_sem=send_sem.at[which],
            recv_sem=recv_sem.at[which],
            device_id=device,
            device_id_type=MESH,
        )

    halo = remote(
        signal_ref.at[:, :, pl.ds(length - width, width)],
        halo_ref,
        0,
        (lax.rem(slab + 1, slabs), me),
    )

    @pl.when(has_next)
    def _():
        halo.start()

    def block_of(ref, group):
        return ref.at[
            group // per_row, :, pl.ds(pl.multiple_of(lax.rem(group, per_row) * patch, patch), patch)
        ]

    def rows_of(ref, member):
        return ref.at[pl.ds(pl.multiple_of(member * contacts, contacts), contacts)]

    def send_tokens(peer):
        remote(
            block_of(filtered_ref, peer), rows_of(tokens_ref, me), 2, (slab, peer)
        ).start()

    def send_ready(step, carry):
        peer = lax.rem(me + step, members)

        @pl.when(lax.rem(peer, per_row) != 0)
        def _():
            send_tokens(peer)

        return carry

    def send_upstream(step, carry):
        peer = lax.rem(me + step, members)
        remote(
            block_of(cotangent_ref, peer), rows_of(upstream_ref, me), 1, (slab, peer)
        ).start()
        return carry

    lax.fori_loop(1, members, send_ready, 0)
    lax.fori_loop(1, members, send_upstream, 0)
    own_upstream = pltpu.make_async_copy(
        block_of(cotangent_ref, me), rows_of(upstream_ref, me), local_sem.at[0]
    )
    own_upstream.start()

    @pl.when(has_prior)
    def _():
        halo.wait_recv()

    @pl.when(jnp.logical_not(has_prior))
    def _():
        halo_ref[...] = jnp.zeros_like(halo_ref)

    finish_filter(halo_ref, rows_ref, table_ref, before_ref, own_ref, filtered_ref)

    def send_first(step, carry):
        peer = lax.rem(me // per_row + step, batch) * per_row

        @pl.when(peer != me)
        def _():
            send_tokens(peer)

        return carry

    lax.fori_loop(0, batch, send_first, 0)
    own_tokens = pltpu.make_async_copy(
        block_of(filtered_ref, me), rows_of(tokens_ref, me), local_sem.at[1]
    )
    own_tokens.start()
    count_hits(neighbours_ref, alive_ref, coef_ref, hits_ref, columns_ref)

    def all_but_one(ref, which):
        rest = ref.at[pl.ds(0, (members - 1) * contacts)]
        return remote(rest, rest, which, core_peer)

    tokens_copy = all_but_one(tokens_ref, 2)
    upstream_copy = all_but_one(upstream_ref, 1)
    own_tokens.wait()
    tokens_copy.wait_recv()
    project_tokens(tokens_ref, hits_ref, columns_ref, weights, work)
    own_upstream.wait()
    upstream_copy.wait_recv()
    attend(upstream_ref, columns_ref, weights, work)
    weight_grads(grads_ref, upstream_ref, work, grad_scale)

    other_half = pl.ds(pl.multiple_of((1 - core) * half, half), half)
    my_half = pl.ds(pl.multiple_of(core * half, half), half)
    core_out[...] = grads_ref[other_half, :].astype(BF16)
    core_copy = remote(core_out, core_in, 3, core_peer)
    core_copy.start()

    mixed = work["mixed_t"][...].astype(F32).T.astype(BF16)
    attended_ref[...] = nn(mixed, w_out_ref[...]).astype(BF16)

    core_copy.wait_recv()
    plane_sum[...] = grads_ref[my_half, :] + core_in[...].astype(F32)
    plane_out[...] = plane_sum[...].astype(BF16)

    def piece_of(ref, at):
        return ref.at[pl.ds(pl.multiple_of(at * piece, piece), piece)]

    def scatter(step, carry):
        at, device = plane_peer(step)
        remote(piece_of(plane_out, at), plane_in.at[step - 1], 4, device).start()
        return carry

    lax.fori_loop(1, plane, scatter, 0)

    scatter_copy = remote(plane_in, plane_in, 4, core_peer)
    scatter_copy.wait_recv()
    running = piece_of(plane_sum, spot)[...]
    for step in range(1, plane):
        running = running + plane_in[step - 1].astype(F32)
    depth_in[level] = running.astype(BF16)

    def exchange(step, carry):
        remote(depth_in.at[level], depth_in.at[level], 6, depth_peer(step)).start()
        return carry

    lax.fori_loop(1, depth, exchange, 0)
    def give_back(step, carry):
        peer = lax.rem(me + step, members)
        remote(
            rows_of(attended_ref, peer), block_of(returned_ref, me), 5, (slab, peer)
        ).start()
        return carry

    lax.fori_loop(1, members, give_back, 0)
    own_back = pltpu.make_async_copy(
        rows_of(attended_ref, me), block_of(returned_ref, me), local_sem.at[0]
    )
    own_back.start()

    rest = depth_in.at[pl.ds(0, depth - 1)]
    depth_copy = remote(rest, rest, 6, core_peer)
    depth_copy.wait_recv()
    running = depth_in[0].astype(F32)
    for at in range(1, depth):
        running = running + depth_in[at].astype(F32)
    own_piece = piece_of(result, spot)
    own_piece[...] = running.astype(BF16)

    def gather(step, carry):
        remote(own_piece, own_piece, 7, plane_peer(step)[1]).start()
        return carry

    lax.fori_loop(1, plane, gather, 0)
    rest = result.at[pl.ds(0, (plane - 1) * piece)]
    gather_copy = remote(rest, rest, 7, core_peer)
    gather_copy.wait_recv()

    last_copy = remote(result, summed_ref.at[my_half], 8, core_peer)
    last_copy.start()
    summed = pltpu.make_async_copy(result, summed_ref.at[my_half], local_sem.at[1])
    summed.start()
    last_copy.wait_recv()

    @pl.when(has_next)
    def _():
        halo.wait_send()

    tokens_copy.wait_send()
    upstream_copy.wait_send()
    core_copy.wait_send()
    scatter_copy.wait_send()
    depth_copy.wait_send()
    gather_copy.wait_send()
    last_copy.wait_send()
    own_back.wait()
    back_copy = all_but_one(attended_ref, 5)
    back_copy.wait_recv()
    back_copy.wait_send()
    summed.wait()


VMEM = pl.BlockSpec(memory_space=pltpu.VMEM)
ANY = pl.BlockSpec(memory_space=pl.ANY)
HBM = pl.BlockSpec(memory_space=pltpu.HBM)


def local(
    signal, fir_taps, neighbours, live_mask, lap_coef, w_query, w_key, w_value, w_out, cotangent
):
    batch, contacts, length = signal.shape
    width = fir_taps.shape[1] - 1
    patch = w_query.shape[0]
    slabs = lax.axis_size("tm")
    members = lax.axis_size("contact")
    tokens = neighbours.shape[0]
    blocks = length // width
    groups = batch * (length // patch) * slabs
    plane = slabs // (CORES * HALVES) * (members // SIDE_LAYERS)
    depth = HALVES * SIDE_LAYERS
    total = 4 * patch
    half = total // CORES
    piece = half // plane
    padded = batch * blocks * contacts
    work = [
        pltpu.VMEM((patch, tokens) if turned else (tokens, patch), dtype)
        for _, turned, dtype in WORK
    ]
    returned, summed = pl.pallas_call(
        functools.partial(step_kernel, slabs, members, (groups * tokens) ** (-0.5)),
        out_shape=(
            jax.ShapeDtypeStruct(signal.shape, BF16),
            jax.ShapeDtypeStruct((total, patch), BF16),
        ),
        in_specs=[HBM] * 10,
        out_specs=(ANY, ANY),
        scratch_shapes=[
            pltpu.VMEM(signal.shape, BF16),
            pltpu.VMEM(fir_taps.shape, BF16),
            pltpu.VMEM((neighbours.shape[1], tokens), jnp.int32),
            pltpu.VMEM((1, tokens), jnp.int32),
            pltpu.VMEM((1, tokens), F32),
            pltpu.VMEM((patch, patch), BF16),
            pltpu.VMEM((patch, patch), BF16),
            pltpu.VMEM((patch, patch), BF16),
            pltpu.VMEM((patch, patch), BF16),
            pltpu.VMEM((batch, contacts, width), BF16),
            pltpu.VMEM((contacts, width, 2 * width), BF16),
            pltpu.VMEM((padded, width), F32),
            pltpu.VMEM((padded, width), F32),
            pltpu.VMEM((padded, width), F32),
            pltpu.VMEM((batch, contacts, length), BF16),
            pltpu.VMEM((tokens, patch), BF16),
            pltpu.VMEM((tokens, patch), BF16),
            pltpu.VMEM((tokens, patch), BF16),
            pltpu.VMEM((tokens, tokens), BF16),
            pltpu.VMEM((4, tokens, 128), F32),
            pltpu.VMEM((total, patch), F32),
            pltpu.VMEM((half, patch), BF16),
            pltpu.VMEM((half, patch), BF16),
            pltpu.VMEM((half, patch), F32),
            pltpu.VMEM((half, patch), BF16),
            pltpu.VMEM((plane - 1, piece, patch), BF16),
            pltpu.VMEM((depth, piece, patch), BF16),
            pltpu.VMEM((half, patch), BF16),
            pltpu.SemaphoreType.DMA((9,)),
            pltpu.SemaphoreType.DMA((9,)),
            pltpu.SemaphoreType.DMA((2,)),
            pltpu.SemaphoreType.DMA((9,)),
        ]
        + work,
        compiler_params=pltpu.CompilerParams(
            collective_id=0, has_side_effects=True, vmem_limit_bytes=VMEM_BYTES
        ),
    )(
        *(
            pltpu.with_memory_space_constraint(array, pltpu.HBM)
            for array in (
                signal,
                fir_taps,
                neighbours.T,
                live_mask.reshape(1, tokens),
                lap_coef.reshape(1, tokens),
                w_query,
                w_key,
                w_value,
                w_out,
                cotangent,
            )
        )
    )
    return (returned, summed.astype(F32).reshape(4, patch, patch))


def solution(mesh):
    in_specs = (
        P(None, "contact", "tm"),
        P("contact", None),
        P(),
        P(),
        P(),
        P(),
        P(),
        P(),
        P(),
        P(None, "contact", "tm"),
    )
    out_specs = (P(None, "contact", "tm"), P())
    return jax.shard_map(local, mesh=mesh, in_specs=in_specs, out_specs=out_specs, check_vma=False)
```

```python
import functools

import jax
import jax.numpy as jnp
from jax import lax
from jax.experimental import pallas as pl
from jax.experimental.pallas import tpu as pltpu
from jax.sharding import PartitionSpec as P

HEADS = 4
CORES = 2
HALVES = 2
SIDE_LAYERS = 4
VMEM_BYTES = 32 * 2**20
MESH = pl.DeviceIdType.MESH
F32 = jnp.float32
BF16 = jnp.bfloat16


def nn(left, right):
    return lax.dot_general(left, right, (((1,), (0,)), ((), ())), preferred_element_type=F32)


def nt(left, right):
    return lax.dot_general(left, right, (((1,), (1,)), ((), ())), preferred_element_type=F32)


def build_tables(taps_ref, table_ref):
    contacts, taps = taps_ref.shape
    width = taps - 1
    values = taps_ref[...].astype(F32)
    source = lax.broadcasted_iota(jnp.int32, (width, width), 0)
    target = lax.broadcasted_iota(jnp.int32, (width, width), 1)
    for c in range(contacts):
        row = jnp.broadcast_to(values[c : c + 1, :width], (width, width))
        turned = pltpu.roll(row, 0, 1, stride=1, stride_axis=0)
        last = jnp.broadcast_to(values[c : c + 1, width:], (width, width))
        own = jnp.where(target >= source, turned, 0.0)
        before = jnp.where(target < source, turned, jnp.where(target == source, last, 0.0))
        table_ref[c, :, :width] = before.astype(BF16)
        table_ref[c, :, width:] = own.astype(BF16)


def spread_blocks(signal_ref, rows_ref, width):
    batch, contacts, length = signal_ref.shape
    blocks = length // width
    for b in range(batch):
        for j in range(blocks):
            at = (b * blocks + j) * contacts
            rows_ref[at : at + contacts, :] = signal_ref[
                b, :, j * width : (j + 1) * width
            ].astype(F32)


def run_filter(rows_ref, table_ref, before_ref, own_ref, filtered_ref):
    batch, contacts, length = filtered_ref.shape
    width = table_ref.shape[1]
    blocks = length // width
    count = batch * blocks
    for c in range(contacts):
        picked = rows_ref[pl.ds(c, count, stride=contacts), :].astype(BF16)
        both = nn(picked, table_ref[c])
        before_ref[pl.ds(c, count, stride=contacts), :] = both[:, :width]
        own_ref[pl.ds(c, count, stride=contacts), :] = both[:, width:]
    for b in range(batch):
        for j in range(1, blocks):
            at = (b * blocks + j) * contacts
            filtered_ref[b, :, j * width : (j + 1) * width] = (
                before_ref[at - contacts : at, :] + own_ref[at : at + contacts, :]
            ).astype(BF16)


def finish_filter(halo_ref, rows_ref, table_ref, before_ref, own_ref, filtered_ref):
    batch, contacts, length = filtered_ref.shape
    width = table_ref.shape[1]
    blocks = length // width
    for b in range(batch):
        rows_ref[b * contacts : (b + 1) * contacts, :] = halo_ref[b].astype(F32)
    for c in range(contacts):
        picked = rows_ref[pl.ds(c, batch, stride=contacts), :].astype(BF16)
        before_ref[pl.ds(c, batch, stride=contacts), :] = nn(picked, table_ref[c, :, :width])
    for b in range(batch):
        at = b * blocks * contacts
        filtered_ref[b, :, :width] = (
            before_ref[b * contacts : (b + 1) * contacts, :] + own_ref[at : at + contacts, :]
        ).astype(BF16)


def count_hits(neighbours_ref, alive_ref, coef_ref, hits_ref, columns_ref):
    slots, tokens = neighbours_ref.shape
    alive_row = alive_ref[...].astype(F32)
    stacked = jnp.concatenate(
        [neighbours_ref[...].astype(F32), alive_row, coef_ref[...]]
        + [jnp.zeros((8 - slots - 2, tokens), F32)],
        axis=0,
    )
    columns = stacked.T
    step = 128
    for at in range(0, tokens, step):
        ids = lax.broadcasted_iota(jnp.int32, (step, tokens), 1).astype(F32)
        hits = jnp.zeros((step, tokens), F32)
        for k in range(slots):
            hits = hits + jnp.where(columns[at : at + step, k : k + 1] == ids, alive_row, 0.0)
        hits_ref[at : at + step, :] = hits.astype(BF16)
        total = jnp.sum(hits, axis=1, keepdims=True)
        columns_ref[0, at : at + step, :] = jnp.broadcast_to(total, (step, 128))
    alive = columns[:, slots : slots + 1]
    columns_ref[1] = jnp.broadcast_to(alive, (tokens, 128))
    columns_ref[2] = jnp.broadcast_to(columns[:, slots + 1 : slots + 2], (tokens, 128))
    columns_ref[3] = jnp.broadcast_to(jnp.where(alive > 0, 0.0, -1e30), (tokens, 128))


def wide(column, lanes):
    return jnp.concatenate([column] * (lanes // column.shape[1]), axis=1)


def project_tokens(tokens_ref, hits_ref, columns_ref, weights, work):
    w_query_ref, w_key_ref, w_value_ref, _ = weights
    tokens, patch = tokens_ref.shape
    middle = tokens_ref[...]
    beside = nn(hits_ref[...], middle)
    middle = middle.astype(F32)
    alive_count, alive, coef = [wide(columns_ref[k], patch) for k in range(3)]
    ready = (alive * (middle + coef * (beside - alive_count * middle))).astype(BF16).astype(F32)
    mean = jnp.sum(ready * ready, axis=1, keepdims=True) * (1.0 / patch)
    normed_f = ready * lax.rsqrt(mean + 1e-05)
    normed = normed_f.astype(BF16)
    work["normed_t"][...] = normed_f.T.astype(BF16)
    score_scale = (patch // HEADS) ** (-0.5)
    query = nn(normed, w_query_ref[...]).astype(BF16).astype(F32)
    work["query"][...] = (query * score_scale).astype(BF16)
    keys = nn(normed, w_key_ref[...]).astype(BF16)
    work["key"][...] = keys
    work["key_t"][...] = keys.astype(F32).T.astype(BF16)
    values = nn(normed, w_value_ref[...]).astype(BF16)
    work["value"][...] = values
    work["value_t"][...] = values.astype(F32).T.astype(BF16)


def head_slices(patch, h):
    head = patch // HEADS
    pair = 2 * head
    return slice(h // 2 * pair, h // 2 * pair + pair), slice(h * head, (h + 1) * head)


def one_of_pair(ref, h):
    tokens, patch = ref.shape
    head = patch // HEADS
    at, _ = head_slices(patch, h)
    lane = lax.broadcasted_iota(jnp.int32, (tokens, 2 * head), 1)
    inside = lane < head if h % 2 == 0 else lane >= head
    return jnp.where(inside, ref[:, at].astype(F32), 0.0).astype(BF16)


def attend(columns_ref, work):
    tokens, patch = work["key"].shape
    bias = wide(columns_ref[3], tokens)
    for h in range(HEADS):
        at, rows = head_slices(patch, h)
        scores = nt(work["key"][:, at], one_of_pair(work["query"], h)) + bias
        raised = jnp.exp(scores - jnp.max(scores, axis=0, keepdims=True))
        prob = raised * (1.0 / jnp.sum(raised, axis=0, keepdims=True))
        prob_low = prob.astype(BF16)
        work["prob"][h] = prob
        work["prob_low"][h] = prob_low
        work["mixed_t"][rows, :] = nn(work["value_t"][rows, :], prob_low).astype(BF16)


def emit_attended(attended_ref, w_out_ref, work):
    mixed = work["mixed_t"][...].astype(F32).T.astype(BF16)
    attended_ref[...] = nn(mixed, w_out_ref[...]).astype(BF16)


def value_grads(upstream_ref, w_out_ref, work):
    patch = upstream_ref.shape[1]
    back = nt(upstream_ref[...], w_out_ref[...]).astype(BF16)
    work["back"][...] = back
    back_t = back.astype(F32).T
    for h in range(0, HEADS, 2):
        at, _ = head_slices(patch, h)
        total = None
        for one in (h, h + 1):
            _, rows = head_slices(patch, one)
            work["inner"][one] = jnp.sum(
                back_t[rows] * work["mixed_t"][rows, :].astype(F32), axis=0, keepdims=True
            )
            part = nn(work["prob_low"][one], one_of_pair(work["back"], one))
            total = part if total is None else total + part
        work["grad_value"][:, at] = total.astype(BF16)


def score_grads(pair, work):
    tokens, patch = work["key"].shape
    score_scale = (patch // HEADS) ** (-0.5)
    total = None
    for h in (2 * pair, 2 * pair + 1):
        at, rows = head_slices(patch, h)
        grad_prob = nt(work["value"][:, at], one_of_pair(work["back"], h))
        grad_score = (work["prob"][h] * (grad_prob - work["inner"][h])).astype(BF16)
        part = nn(grad_score, one_of_pair(work["query"], h))
        total = part if total is None else total + part
        work["grad_query_t"][rows, :] = (
            nn(work["key_t"][rows, :], grad_score) * score_scale
        ).astype(BF16)
    work["grad_key"][:, at] = total.astype(BF16)


def store_grads(grads_ref, products, grad_scale):
    rows = products[0].shape[0]
    pieces, piece = grads_ref.shape[1:3]
    for k, product in enumerate(products):
        grads_ref[k] = (product * grad_scale).reshape(pieces, piece, product.shape[1])


WORK = (
    ("query", 0, BF16),
    ("key", 0, BF16),
    ("value", 0, BF16),
    ("back", 0, BF16),
    ("grad_key", 0, BF16),
    ("grad_value", 0, BF16),
    ("key_t", 1, BF16),
    ("value_t", 1, BF16),
    ("normed_t", 1, BF16),
    ("mixed_t", 1, BF16),
    ("grad_query_t", 1, BF16),
)


def step_kernel(
    slabs,
    members,
    grad_scale,
    signal_hbm,
    taps_hbm,
    neighbours_hbm,
    alive_hbm,
    coef_hbm,
    w_query_hbm,
    w_key_hbm,
    w_value_hbm,
    w_out_hbm,
    cotangent_ref,
    returned_ref,
    summed_ref,
    signal_ref,
    taps_ref,
    neighbours_ref,
    alive_ref,
    coef_ref,
    w_query_ref,
    w_key_ref,
    w_value_ref,
    w_out_ref,
    halo_ref,
    table_ref,
    rows_ref,
    before_ref,
    own_ref,
    filtered_ref,
    tokens_ref,
    upstream_ref,
    attended_ref,
    hits_ref,
    columns_ref,
    grads_ref,
    core_out,
    core_in,
    plane_sum,
    plane_out,
    plane_in,
    depth_in,
    result,
    prob_ref,
    prob_low_ref,
    inner_ref,
    send_sem,
    recv_sem,
    local_sem,
    load_sem,
    *work_refs,
):
    loads = [
        pltpu.make_async_copy(source, target, load_sem.at[k])
        for k, (source, target) in enumerate(
            (
                (signal_hbm, signal_ref),
                (taps_hbm, taps_ref),
                (neighbours_hbm, neighbours_ref),
                (alive_hbm, alive_ref),
                (coef_hbm, coef_ref),
                (w_query_hbm, w_query_ref),
                (w_key_hbm, w_key_ref),
                (w_value_hbm, w_value_ref),
                (w_out_hbm, w_out_ref),
            )
        )
    ]
    for load in loads:
        load.start()
    work = {entry[0]: ref for entry, ref in zip(WORK, work_refs)}
    work["prob"] = prob_ref
    work["prob_low"] = prob_low_ref
    work["inner"] = inner_ref
    weights = (w_query_ref, w_key_ref, w_value_ref, w_out_ref)
    slab = lax.axis_index("tm")
    me = lax.axis_index("contact")
    core = lax.rem(slab, CORES)
    side = lax.rem(slab // CORES, HALVES)
    column = slab // (CORES * HALVES)
    columns = slabs // (CORES * HALVES)
    layers = SIDE_LAYERS
    lines = members // layers
    layer = me // lines
    line = lax.rem(me, lines)
    plane = columns * lines
    depth = HALVES * layers
    spot = column * lines + line
    level = side * layers + layer

    batch, contacts, length = signal_ref.shape
    width = taps_ref.shape[1] - 1
    tokens, patch = tokens_ref.shape
    per_row = length // patch
    has_next = slab < slabs - 1
    has_prior = slab > 0

    def slab_at(column_at, side_at, core_at):
        return (column_at * HALVES + side_at) * CORES + core_at

    core_peer = (slab_at(column, side, 1 - core), me)

    def plane_peer(step):
        at = lax.rem(spot + step, plane)
        return at, (slab_at(at // lines, side, core), layer * lines + lax.rem(at, lines))

    def depth_peer(step):
        at = lax.rem(level + step, depth)
        return slab_at(column, at // layers, core), lax.rem(at, layers) * lines + line

    def contact_peer(step):
        return slab, lax.rem(me + step, members)

    barrier = pltpu.get_barrier_semaphore()

    def greet(device):
        pl.semaphore_signal(barrier, inc=1, device_id=device, device_id_type=MESH)

    def greet_contact(step, carry):
        greet(contact_peer(step))
        return carry

    def greet_plane(step, carry):
        greet(plane_peer(step)[1])
        return carry

    def greet_depth(step, carry):
        greet(depth_peer(step))
        return carry

    @pl.when(has_next)
    def _():
        greet((slab + 1, me))

    @pl.when(has_prior)
    def _():
        greet((slab - 1, me))

    lax.fori_loop(1, members, greet_contact, 0)
    lax.fori_loop(1, plane, greet_plane, 0)
    lax.fori_loop(1, depth, greet_depth, 0)
    greet(core_peer)

    for load in loads:
        load.wait()
    build_tables(taps_ref, table_ref)
    spread_blocks(signal_ref, rows_ref, width)
    run_filter(rows_ref, table_ref, before_ref, own_ref, filtered_ref)

    greetings = members + plane + depth - 2 + has_next.astype(jnp.int32)
    pl.semaphore_wait(barrier, greetings + has_prior.astype(jnp.int32))

    def remote(source, target, which, device):
        return pltpu.make_async_remote_copy(
            src_ref=source,
            dst_ref=target,
            send_sem=send_sem.at[which],
            recv_sem=recv_sem.at[which],
            device_id=device,
            device_id_type=MESH,
        )

    halo = remote(
        signal_ref.at[:, :, pl.ds(length - width, width)],
        halo_ref,
        0,
        (lax.rem(slab + 1, slabs), me),
    )

    @pl.when(has_next)
    def _():
        halo.start()

    def block_of(ref, group):
        return ref.at[
            group // per_row, :, pl.ds(pl.multiple_of(lax.rem(group, per_row) * patch, patch), patch)
        ]

    def rows_of(ref, member):
        return ref.at[pl.ds(pl.multiple_of(member * contacts, contacts), contacts)]

    def send_tokens(peer):
        remote(
            block_of(filtered_ref, peer), rows_of(tokens_ref, me), 2, (slab, peer)
        ).start()

    def send_ready(step, carry):
        peer = lax.rem(me + step, members)

        @pl.when(lax.rem(peer, per_row) != 0)
        def _():
            send_tokens(peer)

        return carry

    def send_upstream(step, carry):
        peer = lax.rem(me + step, members)
        remote(
            block_of(cotangent_ref, peer), rows_of(upstream_ref, me), 1, (slab, peer)
        ).start()
        return carry

    early = members // 2
    lax.fori_loop(1, members, send_ready, 0)
    lax.fori_loop(1, early, send_upstream, 0)
    own_upstream = pltpu.make_async_copy(
        block_of(cotangent_ref, me), rows_of(upstream_ref, me), local_sem.at[0]
    )
    own_upstream.start()

    @pl.when(has_prior)
    def _():
        halo.wait_recv()

    @pl.when(jnp.logical_not(has_prior))
    def _():
        halo_ref[...] = jnp.zeros_like(halo_ref)

    finish_filter(halo_ref, rows_ref, table_ref, before_ref, own_ref, filtered_ref)

    def send_first(step, carry):
        peer = lax.rem(me // per_row + step, batch) * per_row

        @pl.when(peer != me)
        def _():
            send_tokens(peer)

        return carry

    lax.fori_loop(0, batch, send_first, 0)
    lax.fori_loop(early, members, send_upstream, 0)
    own_tokens = pltpu.make_async_copy(
        block_of(filtered_ref, me), rows_of(tokens_ref, me), local_sem.at[1]
    )
    own_tokens.start()
    count_hits(neighbours_ref, alive_ref, coef_ref, hits_ref, columns_ref)

    def all_but_one(ref, which):
        rest = ref.at[pl.ds(0, (members - 1) * contacts)]
        return remote(rest, rest, which, core_peer)

    tokens_copy = all_but_one(tokens_ref, 2)
    upstream_copy = all_but_one(upstream_ref, 1)
    own_tokens.wait()
    tokens_copy.wait_recv()
    project_tokens(tokens_ref, hits_ref, columns_ref, weights, work)
    attend(columns_ref, work)
    emit_attended(attended_ref, w_out_ref, work)

    def give_back(step, carry):
        peer = lax.rem(me + step, members)
        remote(
            rows_of(attended_ref, peer), block_of(returned_ref, me), 3, (slab, peer)
        ).start()
        return carry

    lax.fori_loop(1, members, give_back, 0)
    own_back = pltpu.make_async_copy(
        rows_of(attended_ref, me), block_of(returned_ref, me), local_sem.at[2]
    )
    own_back.start()

    def core_copy(part):
        return remote(core_out.at[part], core_in.at[part], 4 + 5 * part, core_peer)

    def scatter_copy(part):
        ref = plane_in.at[part]
        return remote(ref, ref, 5 + 5 * part, core_peer)

    def depth_copy(part):
        rest = depth_in.at[part, pl.ds(0, depth - 1)]
        return remote(rest, rest, 6 + 5 * part, core_peer)

    def gather_copy(part):
        rest = result.at[part, pl.ds(0, plane - 1)]
        return remote(rest, rest, 7 + 5 * part, core_peer)

    def last_copy(part):
        return remote(
            result.at[part], summed_ref.at[part, core], 8 + 5 * part, core_peer
        )

    def own_summed(part):
        return pltpu.make_async_copy(
            result.at[part], summed_ref.at[part, core], local_sem.at[part]
        )

    def start_core(part, products):
        store_grads(grads_ref.at[part], products, grad_scale)
        core_out[part] = grads_ref[part, 1 - core].astype(BF16)
        core_copy(part).start()

    def start_scatter(part):
        core_copy(part).wait_recv()
        both = grads_ref[part, core] + core_in[part].astype(F32)
        plane_sum[part] = both
        plane_out[part] = both.astype(BF16)

        def scatter(step, carry):
            at, device = plane_peer(step)
            remote(
                plane_out.at[part, at], plane_in.at[part, step - 1], 5 + 5 * part, device
            ).start()
            return carry

        lax.fori_loop(1, plane, scatter, 0)

    def start_exchange(part):
        scatter_copy(part).wait_recv()
        running = plane_sum[part, spot]
        for step in range(1, plane):
            running = running + plane_in[part, step - 1].astype(F32)
        depth_in[part, level] = running.astype(BF16)
        own = depth_in.at[part, level]

        def exchange(step, carry):
            remote(own, own, 6 + 5 * part, depth_peer(step)).start()
            return carry

        lax.fori_loop(1, depth, exchange, 0)

    def start_gather(part):
        depth_copy(part).wait_recv()
        running = depth_in[part, 0].astype(F32)
        for at in range(1, depth):
            running = running + depth_in[part, at].astype(F32)
        result[part, spot] = running.astype(BF16)
        own = result.at[part, spot]

        def gather(step, carry):
            remote(own, own, 7 + 5 * part, plane_peer(step)[1]).start()
            return carry

        lax.fori_loop(1, plane, gather, 0)

    def start_last(part):
        gather_copy(part).wait_recv()
        last_copy(part).start()
        own_summed(part).start()

    own_upstream.wait()
    upstream_copy.wait_recv()
    value_grads(upstream_ref, w_out_ref, work)
    normed_t = work["normed_t"][...]
    start_core(
        1, (nn(normed_t, work["grad_value"][...]), nn(work["mixed_t"][...], upstream_ref[...]))
    )
    score_grads(0, work)
    start_scatter(1)
    score_grads(1, work)
    start_core(
        0, (nt(normed_t, work["grad_query_t"][...]), nn(normed_t, work["grad_key"][...]))
    )
    start_scatter(0)
    start_exchange(1)
    start_exchange(0)
    start_gather(1)
    start_gather(0)
    start_last(1)
    start_last(0)

    @pl.when(has_next)
    def _():
        halo.wait_send()

    tokens_copy.wait_send()
    upstream_copy.wait_send()
    for part in range(2):
        core_copy(part).wait_send()
        scatter_copy(part).wait_send()
        depth_copy(part).wait_send()
        gather_copy(part).wait_send()
        last_copy(part).wait_send()
    own_back.wait()
    back_copy = all_but_one(attended_ref, 3)
    back_copy.wait_recv()
    back_copy.wait_send()
    for part in range(2):
        last_copy(part).wait_recv()
        own_summed(part).wait()


VMEM = pl.BlockSpec(memory_space=pltpu.VMEM)
ANY = pl.BlockSpec(memory_space=pl.ANY)
HBM = pl.BlockSpec(memory_space=pltpu.HBM)


def local(
    signal, fir_taps, neighbours, live_mask, lap_coef, w_query, w_key, w_value, w_out, cotangent
):
    batch, contacts, length = signal.shape
    width = fir_taps.shape[1] - 1
    patch = w_query.shape[0]
    slabs = lax.axis_size("tm")
    members = lax.axis_size("contact")
    tokens = neighbours.shape[0]
    blocks = length // width
    groups = batch * (length // patch) * slabs
    plane = slabs // (CORES * HALVES) * (members // SIDE_LAYERS)
    depth = HALVES * SIDE_LAYERS
    piece = 2 * patch // CORES // plane
    pieces = (2, plane, piece, patch)
    padded = batch * blocks * contacts
    work = [
        pltpu.VMEM((patch, tokens) if turned else (tokens, patch), dtype)
        for _, turned, dtype in WORK
    ]
    returned, summed = pl.pallas_call(
        functools.partial(step_kernel, slabs, members, (groups * tokens) ** (-0.5)),
        out_shape=(
            jax.ShapeDtypeStruct(signal.shape, BF16),
            jax.ShapeDtypeStruct((2, CORES, plane, piece, patch), BF16),
        ),
        in_specs=[HBM] * 10,
        out_specs=(ANY, ANY),
        scratch_shapes=[
            pltpu.VMEM(signal.shape, BF16),
            pltpu.VMEM(fir_taps.shape, BF16),
            pltpu.VMEM((neighbours.shape[1], tokens), jnp.int32),
            pltpu.VMEM((1, tokens), jnp.int32),
            pltpu.VMEM((1, tokens), F32),
            pltpu.VMEM((patch, patch), BF16),
            pltpu.VMEM((patch, patch), BF16),
            pltpu.VMEM((patch, patch), BF16),
            pltpu.VMEM((patch, patch), BF16),
            pltpu.VMEM((batch, contacts, width), BF16),
            pltpu.VMEM((contacts, width, 2 * width), BF16),
            pltpu.VMEM((padded, width), F32),
            pltpu.VMEM((padded, width), F32),
            pltpu.VMEM((padded, width), F32),
            pltpu.VMEM((batch, contacts, length), BF16),
            pltpu.VMEM((tokens, patch), BF16),
            pltpu.VMEM((tokens, patch), BF16),
            pltpu.VMEM((tokens, patch), BF16),
            pltpu.VMEM((tokens, tokens), BF16),
            pltpu.VMEM((4, tokens, 128), F32),
            pltpu.VMEM((2, CORES, plane, piece, patch), F32),
            pltpu.VMEM(pieces, BF16),
            pltpu.VMEM(pieces, BF16),
            pltpu.VMEM(pieces, F32),
            pltpu.VMEM(pieces, BF16),
            pltpu.VMEM((2, plane - 1, piece, patch), BF16),
            pltpu.VMEM((2, depth, piece, patch), BF16),
            pltpu.VMEM(pieces, BF16),
            pltpu.VMEM((HEADS, tokens, tokens), F32),
            pltpu.VMEM((HEADS, tokens, tokens), BF16),
            pltpu.VMEM((HEADS, 1, tokens), F32),
            pltpu.SemaphoreType.DMA((14,)),
            pltpu.SemaphoreType.DMA((14,)),
            pltpu.SemaphoreType.DMA((3,)),
            pltpu.SemaphoreType.DMA((9,)),
        ]
        + work,
        compiler_params=pltpu.CompilerParams(
            collective_id=0, has_side_effects=True, vmem_limit_bytes=VMEM_BYTES
        ),
    )(
        *(
            pltpu.with_memory_space_constraint(array, pltpu.HBM)
            for array in (
                signal,
                fir_taps,
                neighbours.T,
                live_mask.reshape(1, tokens),
                lap_coef.reshape(1, tokens),
                w_query,
                w_key,
                w_value,
                w_out,
                cotangent,
            )
        )
    )
    return (returned, summed.astype(F32).reshape(4, patch, patch))


def solution(mesh):
    in_specs = (
        P(None, "contact", "tm"),
        P("contact", None),
        P(),
        P(),
        P(),
        P(),
        P(),
        P(),
        P(),
        P(None, "contact", "tm"),
    )
    out_specs = (P(None, "contact", "tm"), P())
    return jax.shard_map(local, mesh=mesh, in_specs=in_specs, out_specs=out_specs, check_vma=False)
```

```python
import functools

import jax
import jax.numpy as jnp
from jax import lax
from jax.experimental import pallas as pl
from jax.experimental.pallas import tpu as pltpu
from jax.sharding import PartitionSpec as P

HEADS = 4
CORES = 2
HALVES = 2
SIDE_LAYERS = 4
VMEM_BYTES = 32 * 2**20
MESH = pl.DeviceIdType.MESH
F32 = jnp.float32
BF16 = jnp.bfloat16


def nn(left, right):
    return lax.dot_general(left, right, (((1,), (0,)), ((), ())), preferred_element_type=F32)


def nt(left, right):
    return lax.dot_general(left, right, (((1,), (1,)), ((), ())), preferred_element_type=F32)


def build_tables(taps_ref, table_ref):
    contacts, taps = taps_ref.shape
    width = taps - 1
    values = taps_ref[...].astype(F32)
    source = lax.broadcasted_iota(jnp.int32, (width, width), 0)
    target = lax.broadcasted_iota(jnp.int32, (width, width), 1)
    for c in range(contacts):
        row = jnp.broadcast_to(values[c : c + 1, :width], (width, width))
        turned = pltpu.roll(row, 0, 1, stride=1, stride_axis=0)
        last = jnp.broadcast_to(values[c : c + 1, width:], (width, width))
        own = jnp.where(target >= source, turned, 0.0)
        before = jnp.where(target < source, turned, jnp.where(target == source, last, 0.0))
        table_ref[c, :, :width] = before.astype(BF16)
        table_ref[c, :, width:] = own.astype(BF16)


def spread_blocks(signal_ref, rows_ref, width):
    batch, contacts, length = signal_ref.shape
    blocks = length // width
    for b in range(batch):
        for j in range(blocks):
            at = (b * blocks + j) * contacts
            rows_ref[at : at + contacts, :] = signal_ref[
                b, :, j * width : (j + 1) * width
            ].astype(F32)


def run_filter(rows_ref, table_ref, before_ref, own_ref, filtered_ref):
    batch, contacts, length = filtered_ref.shape
    width = table_ref.shape[1]
    blocks = length // width
    count = batch * blocks
    for c in range(contacts):
        picked = rows_ref[pl.ds(c, count, stride=contacts), :].astype(BF16)
        both = nn(picked, table_ref[c])
        before_ref[pl.ds(c, count, stride=contacts), :] = both[:, :width]
        own_ref[pl.ds(c, count, stride=contacts), :] = both[:, width:]
    for b in range(batch):
        for j in range(1, blocks):
            at = (b * blocks + j) * contacts
            filtered_ref[b, :, j * width : (j + 1) * width] = (
                before_ref[at - contacts : at, :] + own_ref[at : at + contacts, :]
            ).astype(BF16)


def finish_filter(halo_ref, rows_ref, table_ref, before_ref, own_ref, filtered_ref):
    batch, contacts, length = filtered_ref.shape
    width = table_ref.shape[1]
    blocks = length // width
    for b in range(batch):
        rows_ref[b * contacts : (b + 1) * contacts, :] = halo_ref[b].astype(F32)
    for c in range(contacts):
        picked = rows_ref[pl.ds(c, batch, stride=contacts), :].astype(BF16)
        before_ref[pl.ds(c, batch, stride=contacts), :] = nn(picked, table_ref[c, :, :width])
    for b in range(batch):
        at = b * blocks * contacts
        filtered_ref[b, :, :width] = (
            before_ref[b * contacts : (b + 1) * contacts, :] + own_ref[at : at + contacts, :]
        ).astype(BF16)


def count_hits(neighbours_ref, alive_ref, coef_ref, hits_ref, columns_ref):
    slots, tokens = neighbours_ref.shape
    alive_row = alive_ref[...].astype(F32)
    stacked = jnp.concatenate(
        [neighbours_ref[...].astype(F32), alive_row, coef_ref[...]]
        + [jnp.zeros((8 - slots - 2, tokens), F32)],
        axis=0,
    )
    columns = stacked.T
    step = 128
    for at in range(0, tokens, step):
        ids = lax.broadcasted_iota(jnp.int32, (step, tokens), 1).astype(F32)
        hits = jnp.zeros((step, tokens), F32)
        for k in range(slots):
            hits = hits + jnp.where(columns[at : at + step, k : k + 1] == ids, alive_row, 0.0)
        hits_ref[at : at + step, :] = hits.astype(BF16)
        total = jnp.sum(hits, axis=1, keepdims=True)
        columns_ref[0, at : at + step, :] = jnp.broadcast_to(total, (step, 128))
    alive = columns[:, slots : slots + 1]
    columns_ref[1] = jnp.broadcast_to(alive, (tokens, 128))
    columns_ref[2] = jnp.broadcast_to(columns[:, slots + 1 : slots + 2], (tokens, 128))
    columns_ref[3] = jnp.broadcast_to(jnp.where(alive > 0, 0.0, -1e30), (tokens, 128))


def wide(column, lanes):
    return jnp.concatenate([column] * (lanes // column.shape[1]), axis=1)


def project_tokens(tokens_ref, hits_ref, columns_ref, weights, work):
    w_query_ref, w_key_ref, w_value_ref, _ = weights
    tokens, patch = tokens_ref.shape
    middle = tokens_ref[...]
    beside = nn(hits_ref[...], middle)
    middle = middle.astype(F32)
    alive_count, alive, coef = [wide(columns_ref[k], patch) for k in range(3)]
    ready = (alive * (middle + coef * (beside - alive_count * middle))).astype(BF16).astype(F32)
    mean = jnp.sum(ready * ready, axis=1, keepdims=True) * (1.0 / patch)
    normed_f = ready * lax.rsqrt(mean + 1e-05)
    normed = normed_f.astype(BF16)
    work["normed"][...] = normed
    score_scale = (patch // HEADS) ** (-0.5)
    query = nn(normed, w_query_ref[...]).astype(BF16).astype(F32)
    work["query"][...] = (query * score_scale).astype(BF16)
    keys = nn(normed, w_key_ref[...]).astype(BF16)
    work["key"][...] = keys
    values = nn(normed, w_value_ref[...]).astype(BF16)
    work["value"][...] = values
    work["value_t"][...] = values.astype(F32).T.astype(BF16)


def head_slices(patch, h):
    head = patch // HEADS
    pair = 2 * head
    return slice(h // 2 * pair, h // 2 * pair + pair), slice(h * head, (h + 1) * head)


def one_of_pair(ref, h):
    tokens, patch = ref.shape
    head = patch // HEADS
    at, _ = head_slices(patch, h)
    lane = lax.broadcasted_iota(jnp.int32, (tokens, 2 * head), 1)
    inside = lane < head if h % 2 == 0 else lane >= head
    return jnp.where(inside, ref[:, at].astype(F32), 0.0).astype(BF16)


def attend(columns_ref, work):
    tokens, patch = work["key"].shape
    bias = wide(columns_ref[3], tokens)
    for h in range(HEADS):
        at, rows = head_slices(patch, h)
        scores = nt(work["key"][:, at], one_of_pair(work["query"], h)) + bias
        raised = jnp.exp(scores - jnp.max(scores, axis=0, keepdims=True))
        prob = raised * (1.0 / jnp.sum(raised, axis=0, keepdims=True))
        prob_low = prob.astype(BF16)
        work["prob"][h] = prob
        work["prob_low"][h] = prob_low
        work["mixed_t"][rows, :] = nn(work["value_t"][rows, :], prob_low).astype(BF16)


def emit_attended(attended_ref, w_out_ref, work):
    mixed = work["mixed_t"][...].astype(F32).T.astype(BF16)
    attended_ref[...] = nn(mixed, w_out_ref[...]).astype(BF16)


def value_grads(upstream_ref, w_out_ref, work):
    patch = upstream_ref.shape[1]
    back = nt(upstream_ref[...], w_out_ref[...]).astype(BF16)
    work["back"][...] = back
    back_t = back.astype(F32).T
    for h in range(0, HEADS, 2):
        at, _ = head_slices(patch, h)
        total = None
        for one in (h, h + 1):
            _, rows = head_slices(patch, one)
            work["inner"][one] = jnp.sum(
                back_t[rows] * work["mixed_t"][rows, :].astype(F32), axis=0, keepdims=True
            )
            part = nn(work["prob_low"][one], one_of_pair(work["back"], one))
            total = part if total is None else total + part
        work["grad_value"][:, at] = total.astype(BF16)


def score_grads(pair, work):
    tokens, patch = work["key"].shape
    score_scale = (patch // HEADS) ** (-0.5)
    total = None
    for h in (2 * pair, 2 * pair + 1):
        at, rows = head_slices(patch, h)
        grad_prob = nt(work["value"][:, at], one_of_pair(work["back"], h))
        grad_score = (work["prob"][h] * (grad_prob - work["inner"][h])).astype(BF16)
        part = nn(grad_score, one_of_pair(work["query"], h))
        total = part if total is None else total + part
        work["grad_query_t"][rows, :] = (
            nn(work["key_t"][rows, :], grad_score) * score_scale
        ).astype(BF16)
    work["grad_key"][:, at] = total.astype(BF16)


def store_grads(grads_ref, products, grad_scale):
    rows = products[0].shape[0]
    pieces, piece = grads_ref.shape[1:3]
    for k, product in enumerate(products):
        grads_ref[k] = (product * grad_scale).reshape(pieces, piece, product.shape[1])


WORK = (
    ("normed", 0, BF16),
    ("query", 0, BF16),
    ("key", 0, BF16),
    ("value", 0, BF16),
    ("back", 0, BF16),
    ("grad_key", 0, BF16),
    ("grad_value", 0, BF16),
    ("key_t", 1, BF16),
    ("value_t", 1, BF16),
    ("normed_t", 1, BF16),
    ("mixed_t", 1, BF16),
    ("grad_query_t", 1, BF16),
)


def step_kernel(
    slabs,
    members,
    grad_scale,
    signal_hbm,
    taps_hbm,
    neighbours_hbm,
    alive_hbm,
    coef_hbm,
    w_query_hbm,
    w_key_hbm,
    w_value_hbm,
    w_out_hbm,
    cotangent_ref,
    returned_ref,
    summed_ref,
    signal_ref,
    taps_ref,
    neighbours_ref,
    alive_ref,
    coef_ref,
    w_query_ref,
    w_key_ref,
    w_value_ref,
    w_out_ref,
    halo_ref,
    table_ref,
    rows_ref,
    before_ref,
    own_ref,
    filtered_ref,
    tokens_ref,
    upstream_ref,
    attended_ref,
    hits_ref,
    columns_ref,
    grads_ref,
    core_out,
    core_in,
    plane_sum,
    plane_out,
    plane_in,
    depth_in,
    result,
    prob_ref,
    prob_low_ref,
    inner_ref,
    send_sem,
    recv_sem,
    local_sem,
    load_sem,
    *work_refs,
):
    loads = [
        pltpu.make_async_copy(source, target, load_sem.at[k])
        for k, (source, target) in enumerate(
            (
                (signal_hbm, signal_ref),
                (taps_hbm, taps_ref),
                (neighbours_hbm, neighbours_ref),
                (alive_hbm, alive_ref),
                (coef_hbm, coef_ref),
                (w_query_hbm, w_query_ref),
                (w_key_hbm, w_key_ref),
                (w_value_hbm, w_value_ref),
                (w_out_hbm, w_out_ref),
            )
        )
    ]
    for load in loads:
        load.start()
    work = {entry[0]: ref for entry, ref in zip(WORK, work_refs)}
    work["prob"] = prob_ref
    work["prob_low"] = prob_low_ref
    work["inner"] = inner_ref
    weights = (w_query_ref, w_key_ref, w_value_ref, w_out_ref)
    slab = lax.axis_index("tm")
    me = lax.axis_index("contact")
    core = lax.rem(slab, CORES)
    side = lax.rem(slab // CORES, HALVES)
    column = slab // (CORES * HALVES)
    columns = slabs // (CORES * HALVES)
    layers = SIDE_LAYERS
    lines = members // layers
    layer = me // lines
    line = lax.rem(me, lines)
    plane = columns * lines
    depth = HALVES * layers
    spot = column * lines + line
    level = side * layers + layer

    batch, contacts, length = signal_ref.shape
    width = taps_ref.shape[1] - 1
    tokens, patch = tokens_ref.shape
    per_row = length // patch
    has_next = slab < slabs - 1
    has_prior = slab > 0

    def slab_at(column_at, side_at, core_at):
        return (column_at * HALVES + side_at) * CORES + core_at

    core_peer = (slab_at(column, side, 1 - core), me)

    def plane_peer(step):
        at = lax.rem(spot + step, plane)
        return at, (slab_at(at // lines, side, core), layer * lines + lax.rem(at, lines))

    def depth_peer(step):
        at = lax.rem(level + step, depth)
        return slab_at(column, at // layers, core), lax.rem(at, layers) * lines + line

    def contact_peer(step):
        return slab, lax.rem(me + step, members)

    barrier = pltpu.get_barrier_semaphore()

    def greet(device):
        pl.semaphore_signal(barrier, inc=1, device_id=device, device_id_type=MESH)

    def greet_contact(step, carry):
        greet(contact_peer(step))
        return carry

    def greet_plane(step, carry):
        greet(plane_peer(step)[1])
        return carry

    def greet_depth(step, carry):
        greet(depth_peer(step))
        return carry

    @pl.when(has_next)
    def _():
        greet((slab + 1, me))

    @pl.when(has_prior)
    def _():
        greet((slab - 1, me))

    lax.fori_loop(1, members, greet_contact, 0)
    lax.fori_loop(1, plane, greet_plane, 0)
    lax.fori_loop(1, depth, greet_depth, 0)
    greet(core_peer)

    for load in loads:
        load.wait()
    build_tables(taps_ref, table_ref)
    spread_blocks(signal_ref, rows_ref, width)
    run_filter(rows_ref, table_ref, before_ref, own_ref, filtered_ref)

    greetings = members + plane + depth - 2 + has_next.astype(jnp.int32)
    pl.semaphore_wait(barrier, greetings + has_prior.astype(jnp.int32))

    def remote(source, target, which, device):
        return pltpu.make_async_remote_copy(
            src_ref=source,
            dst_ref=target,
            send_sem=send_sem.at[which],
            recv_sem=recv_sem.at[which],
            device_id=device,
            device_id_type=MESH,
        )

    halo = remote(
        signal_ref.at[:, :, pl.ds(length - width, width)],
        halo_ref,
        0,
        (lax.rem(slab + 1, slabs), me),
    )

    @pl.when(has_next)
    def _():
        halo.start()

    def block_of(ref, group):
        return ref.at[
            group // per_row, :, pl.ds(pl.multiple_of(lax.rem(group, per_row) * patch, patch), patch)
        ]

    def rows_of(ref, member):
        return ref.at[pl.ds(pl.multiple_of(member * contacts, contacts), contacts)]

    def send_tokens(peer):
        remote(
            block_of(filtered_ref, peer), rows_of(tokens_ref, me), 2, (slab, peer)
        ).start()

    def send_ready(step, carry):
        peer = lax.rem(me + step, members)

        @pl.when(lax.rem(peer, per_row) != 0)
        def _():
            send_tokens(peer)

        return carry

    def send_upstream(step, carry):
        peer = lax.rem(me + step, members)
        remote(
            block_of(cotangent_ref, peer), rows_of(upstream_ref, me), 1, (slab, peer)
        ).start()
        return carry

    early = 1
    lax.fori_loop(1, members, send_ready, 0)
    lax.fori_loop(1, early, send_upstream, 0)
    own_upstream = pltpu.make_async_copy(
        block_of(cotangent_ref, me), rows_of(upstream_ref, me), local_sem.at[0]
    )
    own_upstream.start()

    @pl.when(has_prior)
    def _():
        halo.wait_recv()

    @pl.when(jnp.logical_not(has_prior))
    def _():
        halo_ref[...] = jnp.zeros_like(halo_ref)

    finish_filter(halo_ref, rows_ref, table_ref, before_ref, own_ref, filtered_ref)

    def send_first(step, carry):
        peer = lax.rem(me // per_row + step, batch) * per_row

        @pl.when(peer != me)
        def _():
            send_tokens(peer)

        return carry

    lax.fori_loop(0, batch, send_first, 0)
    lax.fori_loop(early, members, send_upstream, 0)
    own_tokens = pltpu.make_async_copy(
        block_of(filtered_ref, me), rows_of(tokens_ref, me), local_sem.at[1]
    )
    own_tokens.start()
    count_hits(neighbours_ref, alive_ref, coef_ref, hits_ref, columns_ref)

    def all_but_one(ref, which):
        rest = ref.at[pl.ds(0, (members - 1) * contacts)]
        return remote(rest, rest, which, core_peer)

    tokens_copy = all_but_one(tokens_ref, 2)
    upstream_copy = all_but_one(upstream_ref, 1)
    own_tokens.wait()
    tokens_copy.wait_recv()
    project_tokens(tokens_ref, hits_ref, columns_ref, weights, work)
    attend(columns_ref, work)
    for name in ("normed", "key"):
        work[name + "_t"][...] = work[name][...].astype(F32).T.astype(BF16)

    def core_copy(part):
        return remote(core_out.at[part], core_in.at[part], 4 + 5 * part, core_peer)

    def scatter_copy(part):
        ref = plane_in.at[part]
        return remote(ref, ref, 5 + 5 * part, core_peer)

    def depth_copy(part):
        rest = depth_in.at[part, pl.ds(0, depth - 1)]
        return remote(rest, rest, 6 + 5 * part, core_peer)

    def gather_copy(part):
        rest = result.at[part, pl.ds(0, plane - 1)]
        return remote(rest, rest, 7 + 5 * part, core_peer)

    def last_copy(part):
        return remote(
            result.at[part], summed_ref.at[part, core], 8 + 5 * part, core_peer
        )

    def own_summed(part):
        return pltpu.make_async_copy(
            result.at[part], summed_ref.at[part, core], local_sem.at[part]
        )

    def start_core(part, products):
        store_grads(grads_ref.at[part], products, grad_scale)
        core_out[part] = grads_ref[part, 1 - core].astype(BF16)
        core_copy(part).start()

    def start_scatter(part):
        core_copy(part).wait_recv()
        both = grads_ref[part, core] + core_in[part].astype(F32)
        plane_sum[part] = both
        plane_out[part] = both.astype(BF16)

        def scatter(step, carry):
            at, device = plane_peer(step)
            remote(
                plane_out.at[part, at], plane_in.at[part, step - 1], 5 + 5 * part, device
            ).start()
            return carry

        lax.fori_loop(1, plane, scatter, 0)

    def start_exchange(part):
        scatter_copy(part).wait_recv()
        running = plane_sum[part, spot]
        for step in range(1, plane):
            running = running + plane_in[part, step - 1].astype(F32)
        depth_in[part, level] = running.astype(BF16)
        own = depth_in.at[part, level]

        def exchange(step, carry):
            remote(own, own, 6 + 5 * part, depth_peer(step)).start()
            return carry

        lax.fori_loop(1, depth, exchange, 0)

    def start_gather(part):
        depth_copy(part).wait_recv()
        running = depth_in[part, 0].astype(F32)
        for at in range(1, depth):
            running = running + depth_in[part, at].astype(F32)
        result[part, spot] = running.astype(BF16)
        own = result.at[part, spot]

        def gather(step, carry):
            remote(own, own, 7 + 5 * part, plane_peer(step)[1]).start()
            return carry

        lax.fori_loop(1, plane, gather, 0)

    def start_last(part):
        gather_copy(part).wait_recv()
        last_copy(part).start()
        own_summed(part).start()

    own_upstream.wait()
    upstream_copy.wait_recv()
    value_grads(upstream_ref, w_out_ref, work)
    normed_t = work["normed_t"][...]
    start_core(
        1, (nn(normed_t, work["grad_value"][...]), nn(work["mixed_t"][...], upstream_ref[...]))
    )
    score_grads(0, work)
    start_scatter(1)
    score_grads(1, work)
    start_core(
        0, (nt(normed_t, work["grad_query_t"][...]), nn(normed_t, work["grad_key"][...]))
    )
    start_scatter(0)
    emit_attended(attended_ref, w_out_ref, work)
    start_exchange(1)
    start_exchange(0)
    def give_back(step, carry):
        peer = lax.rem(me + step, members)
        remote(
            rows_of(attended_ref, peer), block_of(returned_ref, me), 3, (slab, peer)
        ).start()
        return carry

    lax.fori_loop(1, members, give_back, 0)
    own_back = pltpu.make_async_copy(
        rows_of(attended_ref, me), block_of(returned_ref, me), local_sem.at[2]
    )
    own_back.start()

    start_gather(1)
    start_gather(0)
    start_last(1)
    start_last(0)

    @pl.when(has_next)
    def _():
        halo.wait_send()

    tokens_copy.wait_send()
    upstream_copy.wait_send()
    for part in range(2):
        core_copy(part).wait_send()
        scatter_copy(part).wait_send()
        depth_copy(part).wait_send()
        gather_copy(part).wait_send()
        last_copy(part).wait_send()
    own_back.wait()
    back_copy = all_but_one(attended_ref, 3)
    back_copy.wait_recv()
    back_copy.wait_send()
    for part in range(2):
        last_copy(part).wait_recv()
        own_summed(part).wait()


def finish_kernel(returned_ref, summed_ref, out_ref, grads_ref, wide_ref, sems):
    back = pltpu.make_async_copy(returned_ref, out_ref, sems.at[0])
    back.start()
    stores = []
    for k in range(grads_ref.shape[0]):
        part = summed_ref[k // CORES, k % CORES].astype(F32)
        wide_ref[k] = part.reshape(wide_ref.shape[1:])
        stores.append(pltpu.make_async_copy(wide_ref.at[k], grads_ref.at[k], sems.at[1 + k]))
        stores[-1].start()
    for store in stores:
        store.wait()
    back.wait()


VMEM = pl.BlockSpec(memory_space=pltpu.VMEM)
ANY = pl.BlockSpec(memory_space=pl.ANY)
HBM = pl.BlockSpec(memory_space=pltpu.HBM)


def local(
    signal, fir_taps, neighbours, live_mask, lap_coef, w_query, w_key, w_value, w_out, cotangent
):
    batch, contacts, length = signal.shape
    width = fir_taps.shape[1] - 1
    patch = w_query.shape[0]
    slabs = lax.axis_size("tm")
    members = lax.axis_size("contact")
    tokens = neighbours.shape[0]
    blocks = length // width
    groups = batch * (length // patch) * slabs
    plane = slabs // (CORES * HALVES) * (members // SIDE_LAYERS)
    depth = HALVES * SIDE_LAYERS
    piece = 2 * patch // CORES // plane
    pieces = (2, plane, piece, patch)
    padded = batch * blocks * contacts
    work = [
        pltpu.VMEM((patch, tokens) if turned else (tokens, patch), dtype)
        for _, turned, dtype in WORK
    ]
    returned, summed = pl.pallas_call(
        functools.partial(step_kernel, slabs, members, (groups * tokens) ** (-0.5)),
        out_shape=(
            jax.ShapeDtypeStruct(signal.shape, BF16),
            jax.ShapeDtypeStruct((2, CORES, plane, piece, patch), BF16),
        ),
        in_specs=[HBM] * 10,
        out_specs=(ANY, ANY),
        scratch_shapes=[
            pltpu.VMEM(signal.shape, BF16),
            pltpu.VMEM(fir_taps.shape, BF16),
            pltpu.VMEM((neighbours.shape[1], tokens), jnp.int32),
            pltpu.VMEM((1, tokens), jnp.int32),
            pltpu.VMEM((1, tokens), F32),
            pltpu.VMEM((patch, patch), BF16),
            pltpu.VMEM((patch, patch), BF16),
            pltpu.VMEM((patch, patch), BF16),
            pltpu.VMEM((patch, patch), BF16),
            pltpu.VMEM((batch, contacts, width), BF16),
            pltpu.VMEM((contacts, width, 2 * width), BF16),
            pltpu.VMEM((padded, width), F32),
            pltpu.VMEM((padded, width), F32),
            pltpu.VMEM((padded, width), F32),
            pltpu.VMEM((batch, contacts, length), BF16),
            pltpu.VMEM((tokens, patch), BF16),
            pltpu.VMEM((tokens, patch), BF16),
            pltpu.VMEM((tokens, patch), BF16),
            pltpu.VMEM((tokens, tokens), BF16),
            pltpu.VMEM((4, tokens, 128), F32),
            pltpu.VMEM((2, CORES, plane, piece, patch), F32),
            pltpu.VMEM(pieces, BF16),
            pltpu.VMEM(pieces, BF16),
            pltpu.VMEM(pieces, F32),
            pltpu.VMEM(pieces, BF16),
            pltpu.VMEM((2, plane - 1, piece, patch), BF16),
            pltpu.VMEM((2, depth, piece, patch), BF16),
            pltpu.VMEM(pieces, BF16),
            pltpu.VMEM((HEADS, tokens, tokens), F32),
            pltpu.VMEM((HEADS, tokens, tokens), BF16),
            pltpu.VMEM((HEADS, 1, tokens), F32),
            pltpu.SemaphoreType.DMA((14,)),
            pltpu.SemaphoreType.DMA((14,)),
            pltpu.SemaphoreType.DMA((3,)),
            pltpu.SemaphoreType.DMA((9,)),
        ]
        + work,
        compiler_params=pltpu.CompilerParams(
            collective_id=0, has_side_effects=True, vmem_limit_bytes=VMEM_BYTES
        ),
    )(
        *(
            pltpu.with_memory_space_constraint(array, pltpu.HBM)
            for array in (
                signal,
                fir_taps,
                neighbours.T,
                live_mask.reshape(1, tokens),
                lap_coef.reshape(1, tokens),
                w_query,
                w_key,
                w_value,
                w_out,
                cotangent,
            )
        )
    )
    return pl.pallas_call(
        finish_kernel,
        out_shape=(
            jax.ShapeDtypeStruct(signal.shape, BF16),
            jax.ShapeDtypeStruct((4, patch, patch), F32),
        ),
        in_specs=[VMEM, VMEM],
        out_specs=(HBM, HBM),
        scratch_shapes=[pltpu.VMEM((4, patch, patch), F32), pltpu.SemaphoreType.DMA((5,))],
        compiler_params=pltpu.CompilerParams(vmem_limit_bytes=8 * 2**20),
    )(returned, summed)


def solution(mesh):
    in_specs = (
        P(None, "contact", "tm"),
        P("contact", None),
        P(),
        P(),
        P(),
        P(),
        P(),
        P(),
        P(),
        P(None, "contact", "tm"),
    )
    out_specs = (P(None, "contact", "tm"), P())
    return jax.shard_map(local, mesh=mesh, in_specs=in_specs, out_specs=out_specs, check_vma=False)
```

```python
import functools

import jax
import jax.numpy as jnp
from jax import lax
from jax.experimental import pallas as pl
from jax.experimental.pallas import tpu as pltpu
from jax.sharding import PartitionSpec as P

HEADS = 4
CORES = 2
HALVES = 2
SIDE_LAYERS = 4
VMEM_BYTES = 32 * 2**20
MESH = pl.DeviceIdType.MESH
F32 = jnp.float32
BF16 = jnp.bfloat16


def nn(left, right):
    return lax.dot_general(left, right, (((1,), (0,)), ((), ())), preferred_element_type=F32)


def nt(left, right):
    return lax.dot_general(left, right, (((1,), (1,)), ((), ())), preferred_element_type=F32)


def build_tables(taps_ref, table_ref):
    contacts, taps = taps_ref.shape
    width = taps - 1
    values = taps_ref[...].astype(F32)
    source = lax.broadcasted_iota(jnp.int32, (width, width), 0)
    target = lax.broadcasted_iota(jnp.int32, (width, width), 1)
    for c in range(contacts):
        row = jnp.broadcast_to(values[c : c + 1, :width], (width, width))
        turned = pltpu.roll(row, 0, 1, stride=1, stride_axis=0)
        last = jnp.broadcast_to(values[c : c + 1, width:], (width, width))
        own = jnp.where(target >= source, turned, 0.0)
        before = jnp.where(target < source, turned, jnp.where(target == source, last, 0.0))
        table_ref[c, :, :width] = before.astype(BF16)
        table_ref[c, :, width:] = own.astype(BF16)


def spread_blocks(signal_ref, rows_ref, width):
    batch, contacts, length = signal_ref.shape
    blocks = length // width
    for b in range(batch):
        for j in range(blocks):
            at = (b * blocks + j) * contacts
            rows_ref[at : at + contacts, :] = signal_ref[
                b, :, j * width : (j + 1) * width
            ].astype(F32)


def run_filter(rows_ref, table_ref, before_ref, own_ref, filtered_ref):
    batch, contacts, length = filtered_ref.shape
    width = table_ref.shape[1]
    blocks = length // width
    count = batch * blocks
    for c in range(contacts):
        picked = rows_ref[pl.ds(c, count, stride=contacts), :].astype(BF16)
        both = nn(picked, table_ref[c])
        before_ref[pl.ds(c, count, stride=contacts), :] = both[:, :width]
        own_ref[pl.ds(c, count, stride=contacts), :] = both[:, width:]
    for b in range(batch):
        for j in range(1, blocks):
            at = (b * blocks + j) * contacts
            filtered_ref[b, :, j * width : (j + 1) * width] = (
                before_ref[at - contacts : at, :] + own_ref[at : at + contacts, :]
            ).astype(BF16)


def finish_filter(halo_ref, rows_ref, table_ref, before_ref, own_ref, filtered_ref):
    batch, contacts, length = filtered_ref.shape
    width = table_ref.shape[1]
    blocks = length // width
    for b in range(batch):
        rows_ref[b * contacts : (b + 1) * contacts, :] = halo_ref[b].astype(F32)
    for c in range(contacts):
        picked = rows_ref[pl.ds(c, batch, stride=contacts), :].astype(BF16)
        before_ref[pl.ds(c, batch, stride=contacts), :] = nn(picked, table_ref[c, :, :width])
    for b in range(batch):
        at = b * blocks * contacts
        filtered_ref[b, :, :width] = (
            before_ref[b * contacts : (b + 1) * contacts, :] + own_ref[at : at + contacts, :]
        ).astype(BF16)


def count_hits(neighbours_ref, alive_ref, coef_ref, hits_ref, columns_ref):
    slots, tokens = neighbours_ref.shape
    alive_row = alive_ref[...].astype(F32)
    stacked = jnp.concatenate(
        [neighbours_ref[...].astype(F32), alive_row, coef_ref[...]]
        + [jnp.zeros((8 - slots - 2, tokens), F32)],
        axis=0,
    )
    columns = stacked.T
    step = 128
    for at in range(0, tokens, step):
        ids = lax.broadcasted_iota(jnp.int32, (step, tokens), 1).astype(F32)
        hits = jnp.zeros((step, tokens), F32)
        for k in range(slots):
            hits = hits + jnp.where(columns[at : at + step, k : k + 1] == ids, alive_row, 0.0)
        hits_ref[at : at + step, :] = hits.astype(BF16)
        total = jnp.sum(hits, axis=1, keepdims=True)
        columns_ref[0, at : at + step, :] = jnp.broadcast_to(total, (step, 128))
    alive = columns[:, slots : slots + 1]
    columns_ref[1] = jnp.broadcast_to(alive, (tokens, 128))
    columns_ref[2] = jnp.broadcast_to(columns[:, slots + 1 : slots + 2], (tokens, 128))
    columns_ref[3] = jnp.broadcast_to(jnp.where(alive > 0, 0.0, -1e30), (tokens, 128))


def wide(column, lanes):
    return jnp.concatenate([column] * (lanes // column.shape[1]), axis=1)


def project_tokens(tokens_ref, hits_ref, columns_ref, weights, work):
    w_query_ref, w_key_ref, w_value_ref, _ = weights
    tokens, patch = tokens_ref.shape
    middle = tokens_ref[...]
    beside = nn(hits_ref[...], middle)
    middle = middle.astype(F32)
    alive_count, alive, coef = [wide(columns_ref[k], patch) for k in range(3)]
    ready = (alive * (middle + coef * (beside - alive_count * middle))).astype(BF16).astype(F32)
    mean = jnp.sum(ready * ready, axis=1, keepdims=True) * (1.0 / patch)
    normed_f = ready * lax.rsqrt(mean + 1e-05)
    normed = normed_f.astype(BF16)
    work["normed"][...] = normed
    score_scale = (patch // HEADS) ** (-0.5)
    query = nn(normed, w_query_ref[...]).astype(BF16).astype(F32)
    work["query"][...] = (query * score_scale).astype(BF16)
    keys = nn(normed, w_key_ref[...]).astype(BF16)
    work["key"][...] = keys
    values = nn(normed, w_value_ref[...]).astype(BF16)
    work["value"][...] = values
    work["value_t"][...] = values.astype(F32).T.astype(BF16)


def head_slices(patch, h):
    head = patch // HEADS
    pair = 2 * head
    return slice(h // 2 * pair, h // 2 * pair + pair), slice(h * head, (h + 1) * head)


def one_of_pair(ref, h):
    tokens, patch = ref.shape
    head = patch // HEADS
    at, _ = head_slices(patch, h)
    lane = lax.broadcasted_iota(jnp.int32, (tokens, 2 * head), 1)
    inside = lane < head if h % 2 == 0 else lane >= head
    return jnp.where(inside, ref[:, at].astype(F32), 0.0).astype(BF16)


def attend(columns_ref, work):
    tokens, patch = work["key"].shape
    bias = wide(columns_ref[3], tokens)

    def scores_of(h):
        at, _ = head_slices(patch, h)
        return nt(work["key"][:, at], one_of_pair(work["query"], h)) + bias

    ahead = scores_of(0)
    for h in range(HEADS):
        _, rows = head_slices(patch, h)
        scores = ahead
        if h + 1 < HEADS:
            ahead = scores_of(h + 1)
        raised = jnp.exp(scores - jnp.max(scores, axis=0, keepdims=True))
        prob = raised * (1.0 / jnp.sum(raised, axis=0, keepdims=True))
        prob_low = prob.astype(BF16)
        work["prob"][h] = prob
        work["prob_low"][h] = prob_low
        work["mixed_t"][rows, :] = nn(work["value_t"][rows, :], prob_low).astype(BF16)


def emit_attended(attended_ref, w_out_ref, work):
    mixed = work["mixed_t"][...].astype(F32).T.astype(BF16)
    attended_ref[...] = nn(mixed, w_out_ref[...]).astype(BF16)


def value_grads(upstream_ref, w_out_ref, work):
    patch = upstream_ref.shape[1]
    back = nt(upstream_ref[...], w_out_ref[...]).astype(BF16)
    work["back"][...] = back
    back_t = back.astype(F32).T
    for h in range(0, HEADS, 2):
        at, _ = head_slices(patch, h)
        total = None
        for one in (h, h + 1):
            _, rows = head_slices(patch, one)
            work["inner"][one] = jnp.sum(
                back_t[rows] * work["mixed_t"][rows, :].astype(F32), axis=0, keepdims=True
            )
            part = nn(work["prob_low"][one], one_of_pair(work["back"], one))
            total = part if total is None else total + part
        work["grad_value"][:, at] = total.astype(BF16)


def score_grads(pair, work):
    tokens, patch = work["key"].shape
    score_scale = (patch // HEADS) ** (-0.5)
    total = None
    for h in (2 * pair, 2 * pair + 1):
        at, rows = head_slices(patch, h)
        grad_prob = nt(work["value"][:, at], one_of_pair(work["back"], h))
        grad_score = (work["prob"][h] * (grad_prob - work["inner"][h])).astype(BF16)
        part = nn(grad_score, one_of_pair(work["query"], h))
        total = part if total is None else total + part
        work["grad_query_t"][rows, :] = (
            nn(work["key_t"][rows, :], grad_score) * score_scale
        ).astype(BF16)
    work["grad_key"][:, at] = total.astype(BF16)


def store_grads(grads_ref, products, grad_scale):
    rows = products[0].shape[0]
    pieces, piece = grads_ref.shape[1:3]
    for k, product in enumerate(products):
        grads_ref[k] = (product * grad_scale).reshape(pieces, piece, product.shape[1])


WORK = (
    ("normed", 0, BF16),
    ("query", 0, BF16),
    ("key", 0, BF16),
    ("value", 0, BF16),
    ("back", 0, BF16),
    ("grad_key", 0, BF16),
    ("grad_value", 0, BF16),
    ("key_t", 1, BF16),
    ("value_t", 1, BF16),
    ("normed_t", 1, BF16),
    ("mixed_t", 1, BF16),
    ("grad_query_t", 1, BF16),
)


def step_kernel(
    slabs,
    members,
    grad_scale,
    signal_hbm,
    taps_hbm,
    neighbours_hbm,
    alive_hbm,
    coef_hbm,
    w_query_hbm,
    w_key_hbm,
    w_value_hbm,
    w_out_hbm,
    cotangent_ref,
    returned_ref,
    summed_ref,
    signal_ref,
    taps_ref,
    neighbours_ref,
    alive_ref,
    coef_ref,
    w_query_ref,
    w_key_ref,
    w_value_ref,
    w_out_ref,
    halo_ref,
    table_ref,
    rows_ref,
    before_ref,
    own_ref,
    filtered_ref,
    tokens_ref,
    upstream_ref,
    attended_ref,
    hits_ref,
    columns_ref,
    grads_ref,
    core_out,
    core_in,
    plane_sum,
    plane_out,
    plane_in,
    depth_in,
    result,
    prob_ref,
    prob_low_ref,
    inner_ref,
    send_sem,
    recv_sem,
    local_sem,
    load_sem,
    *work_refs,
):
    loads = [
        pltpu.make_async_copy(source, target, load_sem.at[k])
        for k, (source, target) in enumerate(
            (
                (signal_hbm, signal_ref),
                (taps_hbm, taps_ref),
                (neighbours_hbm, neighbours_ref),
                (alive_hbm, alive_ref),
                (coef_hbm, coef_ref),
                (w_query_hbm, w_query_ref),
                (w_key_hbm, w_key_ref),
                (w_value_hbm, w_value_ref),
                (w_out_hbm, w_out_ref),
            )
        )
    ]
    for load in loads:
        load.start()
    work = {entry[0]: ref for entry, ref in zip(WORK, work_refs)}
    work["prob"] = prob_ref
    work["prob_low"] = prob_low_ref
    work["inner"] = inner_ref
    weights = (w_query_ref, w_key_ref, w_value_ref, w_out_ref)
    slab = lax.axis_index("tm")
    me = lax.axis_index("contact")
    core = lax.rem(slab, CORES)
    side = lax.rem(slab // CORES, HALVES)
    column = slab // (CORES * HALVES)
    columns = slabs // (CORES * HALVES)
    layers = SIDE_LAYERS
    lines = members // layers
    layer = me // lines
    line = lax.rem(me, lines)
    plane = columns * lines
    depth = HALVES * layers
    spot = column * lines + line
    level = side * layers + layer

    batch, contacts, length = signal_ref.shape
    width = taps_ref.shape[1] - 1
    tokens, patch = tokens_ref.shape
    per_row = length // patch
    has_next = slab < slabs - 1
    has_prior = slab > 0

    def slab_at(column_at, side_at, core_at):
        return (column_at * HALVES + side_at) * CORES + core_at

    core_peer = (slab_at(column, side, 1 - core), me)

    def plane_peer(step):
        at = lax.rem(spot + step, plane)
        return at, (slab_at(at // lines, side, core), layer * lines + lax.rem(at, lines))

    def depth_peer(step):
        at = lax.rem(level + step, depth)
        return slab_at(column, at // layers, core), lax.rem(at, layers) * lines + line

    def contact_peer(step):
        return slab, lax.rem(me + step, members)

    barrier = pltpu.get_barrier_semaphore()

    def greet(device):
        pl.semaphore_signal(barrier, inc=1, device_id=device, device_id_type=MESH)

    def greet_contact(step, carry):
        greet(contact_peer(step))
        return carry

    def greet_plane(step, carry):
        greet(plane_peer(step)[1])
        return carry

    def greet_depth(step, carry):
        greet(depth_peer(step))
        return carry

    @pl.when(has_next)
    def _():
        greet((slab + 1, me))

    @pl.when(has_prior)
    def _():
        greet((slab - 1, me))

    lax.fori_loop(1, members, greet_contact, 0)
    lax.fori_loop(1, plane, greet_plane, 0)
    lax.fori_loop(1, depth, greet_depth, 0)
    greet(core_peer)

    for load in loads:
        load.wait()
    build_tables(taps_ref, table_ref)
    spread_blocks(signal_ref, rows_ref, width)
    run_filter(rows_ref, table_ref, before_ref, own_ref, filtered_ref)

    greetings = members + plane + depth - 2 + has_next.astype(jnp.int32)
    pl.semaphore_wait(barrier, greetings + has_prior.astype(jnp.int32))

    def remote(source, target, which, device):
        return pltpu.make_async_remote_copy(
            src_ref=source,
            dst_ref=target,
            send_sem=send_sem.at[which],
            recv_sem=recv_sem.at[which],
            device_id=device,
            device_id_type=MESH,
        )

    halo = remote(
        signal_ref.at[:, :, pl.ds(length - width, width)],
        halo_ref,
        0,
        (lax.rem(slab + 1, slabs), me),
    )

    @pl.when(has_next)
    def _():
        halo.start()

    def block_of(ref, group):
        return ref.at[
            group // per_row, :, pl.ds(pl.multiple_of(lax.rem(group, per_row) * patch, patch), patch)
        ]

    def rows_of(ref, member):
        return ref.at[pl.ds(pl.multiple_of(member * contacts, contacts), contacts)]

    def send_tokens(peer):
        remote(
            block_of(filtered_ref, peer), rows_of(tokens_ref, me), 2, (slab, peer)
        ).start()

    def send_ready(step, carry):
        peer = lax.rem(me + step, members)

        @pl.when(lax.rem(peer, per_row) != 0)
        def _():
            send_tokens(peer)

        return carry

    def send_upstream(step, carry):
        peer = lax.rem(me + step, members)
        remote(
            block_of(cotangent_ref, peer), rows_of(upstream_ref, me), 1, (slab, peer)
        ).start()
        return carry

    early = 1
    lax.fori_loop(1, members, send_ready, 0)
    lax.fori_loop(1, early, send_upstream, 0)
    own_upstream = pltpu.make_async_copy(
        block_of(cotangent_ref, me), rows_of(upstream_ref, me), local_sem.at[0]
    )
    own_upstream.start()

    @pl.when(has_prior)
    def _():
        halo.wait_recv()

    @pl.when(jnp.logical_not(has_prior))
    def _():
        halo_ref[...] = jnp.zeros_like(halo_ref)

    finish_filter(halo_ref, rows_ref, table_ref, before_ref, own_ref, filtered_ref)

    def send_first(step, carry):
        peer = lax.rem(me // per_row + step, batch) * per_row

        @pl.when(peer != me)
        def _():
            send_tokens(peer)

        return carry

    lax.fori_loop(0, batch, send_first, 0)
    lax.fori_loop(early, members, send_upstream, 0)
    own_tokens = pltpu.make_async_copy(
        block_of(filtered_ref, me), rows_of(tokens_ref, me), local_sem.at[1]
    )
    own_tokens.start()
    count_hits(neighbours_ref, alive_ref, coef_ref, hits_ref, columns_ref)

    def all_but_one(ref, which):
        rest = ref.at[pl.ds(0, (members - 1) * contacts)]
        return remote(rest, rest, which, core_peer)

    tokens_copy = all_but_one(tokens_ref, 2)
    upstream_copy = all_but_one(upstream_ref, 1)
    own_tokens.wait()
    tokens_copy.wait_recv()
    project_tokens(tokens_ref, hits_ref, columns_ref, weights, work)
    attend(columns_ref, work)
    for name in ("normed", "key"):
        work[name + "_t"][...] = work[name][...].astype(F32).T.astype(BF16)

    def core_copy(part):
        return remote(core_out.at[part], core_in.at[part], 4 + 5 * part, core_peer)

    def scatter_copy(part):
        ref = plane_in.at[part]
        return remote(ref, ref, 5 + 5 * part, core_peer)

    def depth_copy(part):
        rest = depth_in.at[part, pl.ds(0, depth - 1)]
        return remote(rest, rest, 6 + 5 * part, core_peer)

    def gather_copy(part):
        rest = result.at[part, pl.ds(0, plane - 1)]
        return remote(rest, rest, 7 + 5 * part, core_peer)

    def last_copy(part):
        return remote(
            result.at[part], summed_ref.at[part, core], 8 + 5 * part, core_peer
        )

    def own_summed(part):
        return pltpu.make_async_copy(
            result.at[part], summed_ref.at[part, core], local_sem.at[part]
        )

    def start_core(part, products):
        store_grads(grads_ref.at[part], products, grad_scale)
        core_out[part] = grads_ref[part, 1 - core].astype(BF16)
        core_copy(part).start()

    def start_scatter(part):
        core_copy(part).wait_recv()
        both = grads_ref[part, core] + core_in[part].astype(F32)
        plane_sum[part] = both
        plane_out[part] = both.astype(BF16)

        def scatter(step, carry):
            at, device = plane_peer(step)
            remote(
                plane_out.at[part, at], plane_in.at[part, step - 1], 5 + 5 * part, device
            ).start()
            return carry

        lax.fori_loop(1, plane, scatter, 0)

    def start_exchange(part):
        scatter_copy(part).wait_recv()
        running = plane_sum[part, spot]
        for step in range(1, plane):
            running = running + plane_in[part, step - 1].astype(F32)
        depth_in[part, level] = running.astype(BF16)
        own = depth_in.at[part, level]

        def exchange(step, carry):
            remote(own, own, 6 + 5 * part, depth_peer(step)).start()
            return carry

        lax.fori_loop(1, depth, exchange, 0)

    def start_gather(part):
        depth_copy(part).wait_recv()
        running = depth_in[part, 0].astype(F32)
        for at in range(1, depth):
            running = running + depth_in[part, at].astype(F32)
        result[part, spot] = running.astype(BF16)
        own = result.at[part, spot]

        def gather(step, carry):
            remote(own, own, 7 + 5 * part, plane_peer(step)[1]).start()
            return carry

        lax.fori_loop(1, plane, gather, 0)

    def start_last(part):
        gather_copy(part).wait_recv()
        last_copy(part).start()
        own_summed(part).start()

    own_upstream.wait()
    upstream_copy.wait_recv()
    value_grads(upstream_ref, w_out_ref, work)
    normed_t = work["normed_t"][...]
    start_core(
        1, (nn(normed_t, work["grad_value"][...]), nn(work["mixed_t"][...], upstream_ref[...]))
    )
    score_grads(0, work)
    start_scatter(1)
    score_grads(1, work)
    start_core(
        0, (nt(normed_t, work["grad_query_t"][...]), nn(normed_t, work["grad_key"][...]))
    )
    start_scatter(0)
    emit_attended(attended_ref, w_out_ref, work)
    start_exchange(1)
    start_exchange(0)
    def give_back(step, carry):
        peer = lax.rem(me + step, members)
        remote(
            rows_of(attended_ref, peer), block_of(returned_ref, me), 3, (slab, peer)
        ).start()
        return carry

    lax.fori_loop(1, members, give_back, 0)
    own_back = pltpu.make_async_copy(
        rows_of(attended_ref, me), block_of(returned_ref, me), local_sem.at[2]
    )
    own_back.start()

    start_gather(1)
    start_gather(0)
    start_last(1)
    start_last(0)

    @pl.when(has_next)
    def _():
        halo.wait_send()

    tokens_copy.wait_send()
    upstream_copy.wait_send()
    for part in range(2):
        core_copy(part).wait_send()
        scatter_copy(part).wait_send()
        depth_copy(part).wait_send()
        gather_copy(part).wait_send()
        last_copy(part).wait_send()
    own_back.wait()
    back_copy = all_but_one(attended_ref, 3)
    back_copy.wait_recv()
    back_copy.wait_send()
    for part in range(2):
        last_copy(part).wait_recv()
        own_summed(part).wait()


def finish_kernel(returned_ref, summed_ref, out_ref, grads_ref, wide_ref, sems):
    back = pltpu.make_async_copy(returned_ref, out_ref, sems.at[0])
    back.start()
    stores = []
    for k in range(grads_ref.shape[0]):
        part = summed_ref[k // CORES, k % CORES].astype(F32)
        wide_ref[k] = part.reshape(wide_ref.shape[1:])
        stores.append(pltpu.make_async_copy(wide_ref.at[k], grads_ref.at[k], sems.at[1 + k]))
        stores[-1].start()
    for store in stores:
        store.wait()
    back.wait()


VMEM = pl.BlockSpec(memory_space=pltpu.VMEM)
ANY = pl.BlockSpec(memory_space=pl.ANY)
HBM = pl.BlockSpec(memory_space=pltpu.HBM)


def local(
    signal, fir_taps, neighbours, live_mask, lap_coef, w_query, w_key, w_value, w_out, cotangent
):
    batch, contacts, length = signal.shape
    width = fir_taps.shape[1] - 1
    patch = w_query.shape[0]
    slabs = lax.axis_size("tm")
    members = lax.axis_size("contact")
    tokens = neighbours.shape[0]
    blocks = length // width
    groups = batch * (length // patch) * slabs
    plane = slabs // (CORES * HALVES) * (members // SIDE_LAYERS)
    depth = HALVES * SIDE_LAYERS
    piece = 2 * patch // CORES // plane
    pieces = (2, plane, piece, patch)
    padded = batch * blocks * contacts
    work = [
        pltpu.VMEM((patch, tokens) if turned else (tokens, patch), dtype)
        for _, turned, dtype in WORK
    ]
    returned, summed = pl.pallas_call(
        functools.partial(step_kernel, slabs, members, (groups * tokens) ** (-0.5)),
        out_shape=(
            jax.ShapeDtypeStruct(signal.shape, BF16),
            jax.ShapeDtypeStruct((2, CORES, plane, piece, patch), BF16),
        ),
        in_specs=[HBM] * 10,
        out_specs=(ANY, ANY),
        scratch_shapes=[
            pltpu.VMEM(signal.shape, BF16),
            pltpu.VMEM(fir_taps.shape, BF16),
            pltpu.VMEM((neighbours.shape[1], tokens), jnp.int32),
            pltpu.VMEM((1, tokens), jnp.int32),
            pltpu.VMEM((1, tokens), F32),
            pltpu.VMEM((patch, patch), BF16),
            pltpu.VMEM((patch, patch), BF16),
            pltpu.VMEM((patch, patch), BF16),
            pltpu.VMEM((patch, patch), BF16),
            pltpu.VMEM((batch, contacts, width), BF16),
            pltpu.VMEM((contacts, width, 2 * width), BF16),
            pltpu.VMEM((padded, width), F32),
            pltpu.VMEM((padded, width), F32),
            pltpu.VMEM((padded, width), F32),
            pltpu.VMEM((batch, contacts, length), BF16),
            pltpu.VMEM((tokens, patch), BF16),
            pltpu.VMEM((tokens, patch), BF16),
            pltpu.VMEM((tokens, patch), BF16),
            pltpu.VMEM((tokens, tokens), BF16),
            pltpu.VMEM((4, tokens, 128), F32),
            pltpu.VMEM((2, CORES, plane, piece, patch), F32),
            pltpu.VMEM(pieces, BF16),
            pltpu.VMEM(pieces, BF16),
            pltpu.VMEM(pieces, F32),
            pltpu.VMEM(pieces, BF16),
            pltpu.VMEM((2, plane - 1, piece, patch), BF16),
            pltpu.VMEM((2, depth, piece, patch), BF16),
            pltpu.VMEM(pieces, BF16),
            pltpu.VMEM((HEADS, tokens, tokens), F32),
            pltpu.VMEM((HEADS, tokens, tokens), BF16),
            pltpu.VMEM((HEADS, 1, tokens), F32),
            pltpu.SemaphoreType.DMA((14,)),
            pltpu.SemaphoreType.DMA((14,)),
            pltpu.SemaphoreType.DMA((3,)),
            pltpu.SemaphoreType.DMA((9,)),
        ]
        + work,
        compiler_params=pltpu.CompilerParams(
            collective_id=0, has_side_effects=True, vmem_limit_bytes=VMEM_BYTES
        ),
    )(
        *(
            pltpu.with_memory_space_constraint(array, pltpu.HBM)
            for array in (
                signal,
                fir_taps,
                neighbours.T,
                live_mask.reshape(1, tokens),
                lap_coef.reshape(1, tokens),
                w_query,
                w_key,
                w_value,
                w_out,
                cotangent,
            )
        )
    )
    return pl.pallas_call(
        finish_kernel,
        out_shape=(
            jax.ShapeDtypeStruct(signal.shape, BF16),
            jax.ShapeDtypeStruct((4, patch, patch), F32),
        ),
        in_specs=[VMEM, VMEM],
        out_specs=(HBM, HBM),
        scratch_shapes=[pltpu.VMEM((4, patch, patch), F32), pltpu.SemaphoreType.DMA((5,))],
        compiler_params=pltpu.CompilerParams(vmem_limit_bytes=8 * 2**20),
    )(returned, summed)


def solution(mesh):
    in_specs = (
        P(None, "contact", "tm"),
        P("contact", None),
        P(),
        P(),
        P(),
        P(),
        P(),
        P(),
        P(),
        P(None, "contact", "tm"),
    )
    out_specs = (P(None, "contact", "tm"), P())
    return jax.shard_map(local, mesh=mesh, in_specs=in_specs, out_specs=out_specs, check_vma=False)
```

```python
import functools

import jax
import jax.numpy as jnp
from jax import lax
from jax.experimental import pallas as pl
from jax.experimental.pallas import tpu as pltpu
from jax.sharding import PartitionSpec as P

HEADS = 4
CORES = 2
HALVES = 2
SIDE_LAYERS = 4
VMEM_BYTES = 32 * 2**20
MESH = pl.DeviceIdType.MESH
F32 = jnp.float32
BF16 = jnp.bfloat16


def nn(left, right):
    return lax.dot_general(left, right, (((1,), (0,)), ((), ())), preferred_element_type=F32)


def nt(left, right):
    return lax.dot_general(left, right, (((1,), (1,)), ((), ())), preferred_element_type=F32)


def build_tables(taps_ref, table_ref):
    contacts, taps = taps_ref.shape
    width = taps - 1
    values = taps_ref[...].astype(F32)
    source = lax.broadcasted_iota(jnp.int32, (width, width), 0)
    target = lax.broadcasted_iota(jnp.int32, (width, width), 1)
    for c in range(contacts):
        row = jnp.broadcast_to(values[c : c + 1, :width], (width, width))
        turned = pltpu.roll(row, 0, 1, stride=1, stride_axis=0)
        last = jnp.broadcast_to(values[c : c + 1, width:], (width, width))
        own = jnp.where(target >= source, turned, 0.0)
        before = jnp.where(target < source, turned, jnp.where(target == source, last, 0.0))
        table_ref[c, :, :width] = before.astype(BF16)
        table_ref[c, :, width:] = own.astype(BF16)


def spread_blocks(signal_ref, rows_ref, width):
    batch, contacts, length = signal_ref.shape
    blocks = length // width
    for b in range(batch):
        for j in range(blocks):
            at = (b * blocks + j) * contacts
            rows_ref[at : at + contacts, :] = signal_ref[
                b, :, j * width : (j + 1) * width
            ].astype(F32)


def run_filter(rows_ref, table_ref, before_ref, own_ref, filtered_ref):
    batch, contacts, length = filtered_ref.shape
    width = table_ref.shape[1]
    blocks = length // width
    count = batch * blocks
    for c in range(contacts):
        picked = rows_ref[pl.ds(c, count, stride=contacts), :].astype(BF16)
        both = nn(picked, table_ref[c])
        before_ref[pl.ds(c, count, stride=contacts), :] = both[:, :width]
        own_ref[pl.ds(c, count, stride=contacts), :] = both[:, width:]
    for b in range(batch):
        for j in range(1, blocks):
            at = (b * blocks + j) * contacts
            filtered_ref[b, :, j * width : (j + 1) * width] = (
                before_ref[at - contacts : at, :] + own_ref[at : at + contacts, :]
            ).astype(BF16)


def finish_filter(halo_ref, rows_ref, table_ref, before_ref, own_ref, filtered_ref):
    batch, contacts, length = filtered_ref.shape
    width = table_ref.shape[1]
    blocks = length // width
    for b in range(batch):
        rows_ref[b * contacts : (b + 1) * contacts, :] = halo_ref[b].astype(F32)
    for c in range(contacts):
        picked = rows_ref[pl.ds(c, batch, stride=contacts), :].astype(BF16)
        before_ref[pl.ds(c, batch, stride=contacts), :] = nn(picked, table_ref[c, :, :width])
    for b in range(batch):
        at = b * blocks * contacts
        filtered_ref[b, :, :width] = (
            before_ref[b * contacts : (b + 1) * contacts, :] + own_ref[at : at + contacts, :]
        ).astype(BF16)


def count_hits(neighbours_ref, alive_ref, coef_ref, hits_ref, columns_ref):
    slots, tokens = neighbours_ref.shape
    alive_row = alive_ref[...].astype(F32)
    stacked = jnp.concatenate(
        [neighbours_ref[...].astype(F32), alive_row, coef_ref[...]]
        + [jnp.zeros((8 - slots - 2, tokens), F32)],
        axis=0,
    )
    columns = stacked.T
    step = 128
    for at in range(0, tokens, step):
        ids = lax.broadcasted_iota(jnp.int32, (step, tokens), 1).astype(F32)
        hits = jnp.zeros((step, tokens), F32)
        for k in range(slots):
            hits = hits + jnp.where(columns[at : at + step, k : k + 1] == ids, alive_row, 0.0)
        hits_ref[at : at + step, :] = hits.astype(BF16)
        total = jnp.sum(hits, axis=1, keepdims=True)
        columns_ref[0, at : at + step, :] = jnp.broadcast_to(total, (step, 128))
    alive = columns[:, slots : slots + 1]
    columns_ref[1] = jnp.broadcast_to(alive, (tokens, 128))
    columns_ref[2] = jnp.broadcast_to(columns[:, slots + 1 : slots + 2], (tokens, 128))
    columns_ref[3] = jnp.broadcast_to(jnp.where(alive > 0, 0.0, -1e30), (tokens, 128))


def wide(column, lanes):
    return jnp.concatenate([column] * (lanes // column.shape[1]), axis=1)


def project_tokens(tokens_ref, hits_ref, columns_ref, weights, work):
    w_query_ref, w_key_ref, w_value_ref, _ = weights
    tokens, patch = tokens_ref.shape
    middle = tokens_ref[...]
    beside = nn(hits_ref[...], middle)
    middle = middle.astype(F32)
    alive_count, alive, coef = [wide(columns_ref[k], patch) for k in range(3)]
    ready = (alive * (middle + coef * (beside - alive_count * middle))).astype(BF16).astype(F32)
    mean = jnp.sum(ready * ready, axis=1, keepdims=True) * (1.0 / patch)
    normed_f = ready * lax.rsqrt(mean + 1e-05)
    normed = normed_f.astype(BF16)
    work["normed"][...] = normed
    score_scale = (patch // HEADS) ** (-0.5)
    query = nn(normed, w_query_ref[...]).astype(BF16).astype(F32)
    work["query"][...] = (query * score_scale).astype(BF16)
    keys = nn(normed, w_key_ref[...]).astype(BF16)
    work["key"][...] = keys
    values = nn(normed, w_value_ref[...]).astype(BF16)
    work["value"][...] = values
    work["value_t"][...] = values.astype(F32).T.astype(BF16)


def head_slices(patch, h):
    head = patch // HEADS
    pair = 2 * head
    return slice(h // 2 * pair, h // 2 * pair + pair), slice(h * head, (h + 1) * head)


def one_of_pair(ref, h):
    tokens, patch = ref.shape
    head = patch // HEADS
    at, _ = head_slices(patch, h)
    lane = lax.broadcasted_iota(jnp.int32, (tokens, 2 * head), 1)
    inside = lane < head if h % 2 == 0 else lane >= head
    return jnp.where(inside, ref[:, at].astype(F32), 0.0).astype(BF16)


def attend(columns_ref, work):
    tokens, patch = work["key"].shape
    bias = wide(columns_ref[3], tokens)

    def scores_of(h):
        at, _ = head_slices(patch, h)
        return nt(work["key"][:, at], one_of_pair(work["query"], h)) + bias

    ahead = scores_of(0)
    for h in range(HEADS):
        _, rows = head_slices(patch, h)
        scores = ahead
        if h + 1 < HEADS:
            ahead = scores_of(h + 1)
        raised = jnp.exp(scores - jnp.max(scores, axis=0, keepdims=True))
        prob = raised * (1.0 / jnp.sum(raised, axis=0, keepdims=True))
        prob_low = prob.astype(BF16)
        work["prob"][h] = prob
        work["prob_low"][h] = prob_low
        work["mixed_t"][rows, :] = nn(work["value_t"][rows, :], prob_low).astype(BF16)


def emit_attended(attended_ref, w_out_ref, work):
    mixed = work["mixed_t"][...].astype(F32).T.astype(BF16)
    attended_ref[...] = nn(mixed, w_out_ref[...]).astype(BF16)


def value_grads(upstream_ref, w_out_ref, work):
    patch = upstream_ref.shape[1]
    back = nt(upstream_ref[...], w_out_ref[...]).astype(BF16)
    work["back"][...] = back
    back_t = back.astype(F32).T
    for h in range(0, HEADS, 2):
        at, _ = head_slices(patch, h)
        total = None
        for one in (h, h + 1):
            _, rows = head_slices(patch, one)
            work["inner"][one] = jnp.sum(
                back_t[rows] * work["mixed_t"][rows, :].astype(F32), axis=0, keepdims=True
            )
            part = nn(work["prob_low"][one], one_of_pair(work["back"], one))
            total = part if total is None else total + part
        work["grad_value"][:, at] = total.astype(BF16)


def score_grads(pair, work):
    tokens, patch = work["key"].shape
    score_scale = (patch // HEADS) ** (-0.5)
    total = None
    for h in (2 * pair, 2 * pair + 1):
        at, rows = head_slices(patch, h)
        grad_prob = nt(work["value"][:, at], one_of_pair(work["back"], h))
        grad_score = (work["prob"][h] * (grad_prob - work["inner"][h])).astype(BF16)
        part = nn(grad_score, one_of_pair(work["query"], h))
        total = part if total is None else total + part
        work["grad_query_t"][rows, :] = (
            nn(work["key_t"][rows, :], grad_score) * score_scale
        ).astype(BF16)
    work["grad_key"][:, at] = total.astype(BF16)


def store_grads(grads_ref, products, grad_scale):
    rows = products[0].shape[0]
    pieces, piece = grads_ref.shape[1:3]
    for k, product in enumerate(products):
        grads_ref[k] = (product * grad_scale).reshape(pieces, piece, product.shape[1])


WORK = (
    ("normed", 0, BF16),
    ("query", 0, BF16),
    ("key", 0, BF16),
    ("value", 0, BF16),
    ("back", 0, BF16),
    ("grad_key", 0, BF16),
    ("grad_value", 0, BF16),
    ("key_t", 1, BF16),
    ("value_t", 1, BF16),
    ("normed_t", 1, BF16),
    ("mixed_t", 1, BF16),
    ("grad_query_t", 1, BF16),
)


def step_kernel(
    slabs,
    members,
    grad_scale,
    signal_hbm,
    taps_hbm,
    neighbours_hbm,
    alive_hbm,
    coef_hbm,
    w_query_hbm,
    w_key_hbm,
    w_value_hbm,
    w_out_hbm,
    cotangent_ref,
    returned_ref,
    summed_ref,
    signal_ref,
    taps_ref,
    neighbours_ref,
    alive_ref,
    coef_ref,
    w_query_ref,
    w_key_ref,
    w_value_ref,
    w_out_ref,
    halo_ref,
    table_ref,
    rows_ref,
    before_ref,
    own_ref,
    filtered_ref,
    tokens_ref,
    upstream_ref,
    attended_ref,
    hits_ref,
    columns_ref,
    grads_ref,
    core_out,
    core_in,
    plane_sum,
    plane_out,
    plane_in,
    depth_in,
    result,
    prob_ref,
    prob_low_ref,
    inner_ref,
    send_sem,
    recv_sem,
    local_sem,
    load_sem,
    *work_refs,
):
    loads = [
        pltpu.make_async_copy(source, target, load_sem.at[k])
        for k, (source, target) in enumerate(
            (
                (signal_hbm, signal_ref),
                (taps_hbm, taps_ref),
                (neighbours_hbm, neighbours_ref),
                (alive_hbm, alive_ref),
                (coef_hbm, coef_ref),
                (w_query_hbm, w_query_ref),
                (w_key_hbm, w_key_ref),
                (w_value_hbm, w_value_ref),
                (w_out_hbm, w_out_ref),
            )
        )
    ]
    for load in loads:
        load.start()
    work = {entry[0]: ref for entry, ref in zip(WORK, work_refs)}
    work["prob"] = prob_ref
    work["prob_low"] = prob_low_ref
    work["inner"] = inner_ref
    weights = (w_query_ref, w_key_ref, w_value_ref, w_out_ref)
    slab = lax.axis_index("tm")
    me = lax.axis_index("contact")
    core = lax.rem(slab, CORES)
    side = lax.rem(slab // CORES, HALVES)
    column = slab // (CORES * HALVES)
    columns = slabs // (CORES * HALVES)
    layers = SIDE_LAYERS
    lines = members // layers
    layer = me // lines
    line = lax.rem(me, lines)
    plane = columns * lines
    depth = HALVES * layers
    spot = column * lines + line
    level = side * layers + layer

    batch, contacts, length = signal_ref.shape
    width = taps_ref.shape[1] - 1
    tokens, patch = tokens_ref.shape
    per_row = length // patch
    has_next = slab < slabs - 1
    has_prior = slab > 0

    def slab_at(column_at, side_at, core_at):
        return (column_at * HALVES + side_at) * CORES + core_at

    core_peer = (slab_at(column, side, 1 - core), me)

    def plane_peer(step):
        at = lax.rem(spot + step, plane)
        return at, (slab_at(at // lines, side, core), layer * lines + lax.rem(at, lines))

    def depth_peer(step):
        at = lax.rem(level + step, depth)
        return slab_at(column, at // layers, core), lax.rem(at, layers) * lines + line

    def contact_peer(step):
        return slab, lax.rem(me + step, members)

    barrier = pltpu.get_barrier_semaphore()

    def greet(device):
        pl.semaphore_signal(barrier, inc=1, device_id=device, device_id_type=MESH)

    def greet_contact(step, carry):
        greet(contact_peer(step))
        return carry

    def greet_plane(step, carry):
        greet(plane_peer(step)[1])
        return carry

    def greet_depth(step, carry):
        greet(depth_peer(step))
        return carry

    @pl.when(has_next)
    def _():
        greet((slab + 1, me))

    @pl.when(has_prior)
    def _():
        greet((slab - 1, me))

    lax.fori_loop(1, members, greet_contact, 0)
    lax.fori_loop(1, plane, greet_plane, 0)
    lax.fori_loop(1, depth, greet_depth, 0)
    greet(core_peer)

    for load in loads:
        load.wait()
    build_tables(taps_ref, table_ref)
    spread_blocks(signal_ref, rows_ref, width)
    run_filter(rows_ref, table_ref, before_ref, own_ref, filtered_ref)

    greetings = members + plane + depth - 2 + has_next.astype(jnp.int32)
    pl.semaphore_wait(barrier, greetings + has_prior.astype(jnp.int32))

    def remote(source, target, which, device):
        return pltpu.make_async_remote_copy(
            src_ref=source,
            dst_ref=target,
            send_sem=send_sem.at[which],
            recv_sem=recv_sem.at[which],
            device_id=device,
            device_id_type=MESH,
        )

    halo = remote(
        signal_ref.at[:, :, pl.ds(length - width, width)],
        halo_ref,
        0,
        (lax.rem(slab + 1, slabs), me),
    )

    @pl.when(has_next)
    def _():
        halo.start()

    def block_of(ref, group):
        return ref.at[
            group // per_row, :, pl.ds(pl.multiple_of(lax.rem(group, per_row) * patch, patch), patch)
        ]

    def rows_of(ref, member):
        return ref.at[pl.ds(pl.multiple_of(member * contacts, contacts), contacts)]

    def send_tokens(peer):
        remote(
            block_of(filtered_ref, peer), rows_of(tokens_ref, me), 2, (slab, peer)
        ).start()

    def send_ready(step, carry):
        peer = lax.rem(me + step, members)

        @pl.when(lax.rem(peer, per_row) != 0)
        def _():
            send_tokens(peer)

        return carry

    def send_upstream(step, carry):
        peer = lax.rem(me + step, members)
        remote(
            block_of(cotangent_ref, peer), rows_of(upstream_ref, me), 1, (slab, peer)
        ).start()
        return carry

    early = members // 4
    lax.fori_loop(1, members, send_ready, 0)
    lax.fori_loop(1, early, send_upstream, 0)
    own_upstream = pltpu.make_async_copy(
        block_of(cotangent_ref, me), rows_of(upstream_ref, me), local_sem.at[0]
    )
    own_upstream.start()

    @pl.when(has_prior)
    def _():
        halo.wait_recv()

    @pl.when(jnp.logical_not(has_prior))
    def _():
        halo_ref[...] = jnp.zeros_like(halo_ref)

    finish_filter(halo_ref, rows_ref, table_ref, before_ref, own_ref, filtered_ref)

    def send_first(step, carry):
        peer = lax.rem(me // per_row + step, batch) * per_row

        @pl.when(peer != me)
        def _():
            send_tokens(peer)

        return carry

    lax.fori_loop(0, batch, send_first, 0)
    lax.fori_loop(early, members, send_upstream, 0)
    own_tokens = pltpu.make_async_copy(
        block_of(filtered_ref, me), rows_of(tokens_ref, me), local_sem.at[1]
    )
    own_tokens.start()
    count_hits(neighbours_ref, alive_ref, coef_ref, hits_ref, columns_ref)

    def all_but_one(ref, which):
        rest = ref.at[pl.ds(0, (members - 1) * contacts)]
        return remote(rest, rest, which, core_peer)

    tokens_copy = all_but_one(tokens_ref, 2)
    upstream_copy = all_but_one(upstream_ref, 1)
    own_tokens.wait()
    tokens_copy.wait_recv()
    project_tokens(tokens_ref, hits_ref, columns_ref, weights, work)
    attend(columns_ref, work)
    for name in ("normed", "key"):
        work[name + "_t"][...] = work[name][...].astype(F32).T.astype(BF16)

    def core_copy(part):
        return remote(core_out.at[part], core_in.at[part], 4 + 5 * part, core_peer)

    def scatter_copy(part):
        ref = plane_in.at[part]
        return remote(ref, ref, 5 + 5 * part, core_peer)

    def depth_copy(part):
        rest = depth_in.at[part, pl.ds(0, depth - 1)]
        return remote(rest, rest, 6 + 5 * part, core_peer)

    def gather_copy(part):
        rest = result.at[part, pl.ds(0, plane - 1)]
        return remote(rest, rest, 7 + 5 * part, core_peer)

    def last_copy(part):
        return remote(
            result.at[part], summed_ref.at[part, core], 8 + 5 * part, core_peer
        )

    def own_summed(part):
        return pltpu.make_async_copy(
            result.at[part], summed_ref.at[part, core], local_sem.at[part]
        )

    def start_core(part, products):
        store_grads(grads_ref.at[part], products, grad_scale)
        core_out[part] = grads_ref[part, 1 - core].astype(BF16)
        core_copy(part).start()

    def start_scatter(part):
        core_copy(part).wait_recv()
        both = grads_ref[part, core] + core_in[part].astype(F32)
        plane_sum[part] = both
        plane_out[part] = both.astype(BF16)

        def scatter(step, carry):
            at, device = plane_peer(step)
            remote(
                plane_out.at[part, at], plane_in.at[part, step - 1], 5 + 5 * part, device
            ).start()
            return carry

        lax.fori_loop(1, plane, scatter, 0)

    def start_exchange(part):
        scatter_copy(part).wait_recv()
        running = plane_sum[part, spot]
        for step in range(1, plane):
            running = running + plane_in[part, step - 1].astype(F32)
        depth_in[part, level] = running.astype(BF16)
        own = depth_in.at[part, level]

        def exchange(step, carry):
            remote(own, own, 6 + 5 * part, depth_peer(step)).start()
            return carry

        lax.fori_loop(1, depth, exchange, 0)

    def start_gather(part):
        depth_copy(part).wait_recv()
        running = depth_in[part, 0].astype(F32)
        for at in range(1, depth):
            running = running + depth_in[part, at].astype(F32)
        result[part, spot] = running.astype(BF16)
        own = result.at[part, spot]

        def gather(step, carry):
            remote(own, own, 7 + 5 * part, plane_peer(step)[1]).start()
            return carry

        lax.fori_loop(1, plane, gather, 0)

    def start_last(part):
        gather_copy(part).wait_recv()
        last_copy(part).start()
        own_summed(part).start()

    own_upstream.wait()
    upstream_copy.wait_recv()
    value_grads(upstream_ref, w_out_ref, work)
    normed_t = work["normed_t"][...]
    start_core(
        1, (nn(normed_t, work["grad_value"][...]), nn(work["mixed_t"][...], upstream_ref[...]))
    )
    score_grads(0, work)
    start_scatter(1)
    score_grads(1, work)
    start_core(
        0, (nt(normed_t, work["grad_query_t"][...]), nn(normed_t, work["grad_key"][...]))
    )
    start_scatter(0)
    emit_attended(attended_ref, w_out_ref, work)
    start_exchange(1)
    start_exchange(0)
    def give_back(step, carry):
        peer = lax.rem(me + step, members)
        remote(
            rows_of(attended_ref, peer), block_of(returned_ref, me), 3, (slab, peer)
        ).start()
        return carry

    lax.fori_loop(1, members, give_back, 0)
    own_back = pltpu.make_async_copy(
        rows_of(attended_ref, me), block_of(returned_ref, me), local_sem.at[2]
    )
    own_back.start()

    start_gather(1)
    start_gather(0)
    start_last(1)
    start_last(0)

    @pl.when(has_next)
    def _():
        halo.wait_send()

    tokens_copy.wait_send()
    upstream_copy.wait_send()
    for part in range(2):
        core_copy(part).wait_send()
        scatter_copy(part).wait_send()
        depth_copy(part).wait_send()
        gather_copy(part).wait_send()
        last_copy(part).wait_send()
    own_back.wait()
    back_copy = all_but_one(attended_ref, 3)
    back_copy.wait_recv()
    back_copy.wait_send()
    for part in range(2):
        last_copy(part).wait_recv()
        own_summed(part).wait()


def finish_kernel(returned_ref, summed_ref, out_ref, grads_ref, wide_ref, sems):
    back = pltpu.make_async_copy(returned_ref, out_ref, sems.at[0])
    back.start()
    stores = []
    for k in range(grads_ref.shape[0]):
        part = summed_ref[k // CORES, k % CORES].astype(F32)
        wide_ref[k] = part.reshape(wide_ref.shape[1:])
        stores.append(pltpu.make_async_copy(wide_ref.at[k], grads_ref.at[k], sems.at[1 + k]))
        stores[-1].start()
    for store in stores:
        store.wait()
    back.wait()


VMEM = pl.BlockSpec(memory_space=pltpu.VMEM)
ANY = pl.BlockSpec(memory_space=pl.ANY)
HBM = pl.BlockSpec(memory_space=pltpu.HBM)


def local(
    signal, fir_taps, neighbours, live_mask, lap_coef, w_query, w_key, w_value, w_out, cotangent
):
    batch, contacts, length = signal.shape
    width = fir_taps.shape[1] - 1
    patch = w_query.shape[0]
    slabs = lax.axis_size("tm")
    members = lax.axis_size("contact")
    tokens = neighbours.shape[0]
    blocks = length // width
    groups = batch * (length // patch) * slabs
    plane = slabs // (CORES * HALVES) * (members // SIDE_LAYERS)
    depth = HALVES * SIDE_LAYERS
    piece = 2 * patch // CORES // plane
    pieces = (2, plane, piece, patch)
    padded = batch * blocks * contacts
    work = [
        pltpu.VMEM((patch, tokens) if turned else (tokens, patch), dtype)
        for _, turned, dtype in WORK
    ]
    returned, summed = pl.pallas_call(
        functools.partial(step_kernel, slabs, members, (groups * tokens) ** (-0.5)),
        out_shape=(
            jax.ShapeDtypeStruct(signal.shape, BF16),
            jax.ShapeDtypeStruct((2, CORES, plane, piece, patch), BF16),
        ),
        in_specs=[HBM] * 10,
        out_specs=(ANY, ANY),
        scratch_shapes=[
            pltpu.VMEM(signal.shape, BF16),
            pltpu.VMEM(fir_taps.shape, BF16),
            pltpu.VMEM((neighbours.shape[1], tokens), jnp.int32),
            pltpu.VMEM((1, tokens), jnp.int32),
            pltpu.VMEM((1, tokens), F32),
            pltpu.VMEM((patch, patch), BF16),
            pltpu.VMEM((patch, patch), BF16),
            pltpu.VMEM((patch, patch), BF16),
            pltpu.VMEM((patch, patch), BF16),
            pltpu.VMEM((batch, contacts, width), BF16),
            pltpu.VMEM((contacts, width, 2 * width), BF16),
            pltpu.VMEM((padded, width), F32),
            pltpu.VMEM((padded, width), F32),
            pltpu.VMEM((padded, width), F32),
            pltpu.VMEM((batch, contacts, length), BF16),
            pltpu.VMEM((tokens, patch), BF16),
            pltpu.VMEM((tokens, patch), BF16),
            pltpu.VMEM((tokens, patch), BF16),
            pltpu.VMEM((tokens, tokens), BF16),
            pltpu.VMEM((4, tokens, 128), F32),
            pltpu.VMEM((2, CORES, plane, piece, patch), F32),
            pltpu.VMEM(pieces, BF16),
            pltpu.VMEM(pieces, BF16),
            pltpu.VMEM(pieces, F32),
            pltpu.VMEM(pieces, BF16),
            pltpu.VMEM((2, plane - 1, piece, patch), BF16),
            pltpu.VMEM((2, depth, piece, patch), BF16),
            pltpu.VMEM(pieces, BF16),
            pltpu.VMEM((HEADS, tokens, tokens), F32),
            pltpu.VMEM((HEADS, tokens, tokens), BF16),
            pltpu.VMEM((HEADS, 1, tokens), F32),
            pltpu.SemaphoreType.DMA((14,)),
            pltpu.SemaphoreType.DMA((14,)),
            pltpu.SemaphoreType.DMA((3,)),
            pltpu.SemaphoreType.DMA((9,)),
        ]
        + work,
        compiler_params=pltpu.CompilerParams(
            collective_id=0, has_side_effects=True, vmem_limit_bytes=VMEM_BYTES
        ),
    )(
        *(
            pltpu.with_memory_space_constraint(array, pltpu.HBM)
            for array in (
                signal,
                fir_taps,
                neighbours.T,
                live_mask.reshape(1, tokens),
                lap_coef.reshape(1, tokens),
                w_query,
                w_key,
                w_value,
                w_out,
                cotangent,
            )
        )
    )
    return pl.pallas_call(
        finish_kernel,
        out_shape=(
            jax.ShapeDtypeStruct(signal.shape, BF16),
            jax.ShapeDtypeStruct((4, patch, patch), F32),
        ),
        in_specs=[VMEM, VMEM],
        out_specs=(HBM, HBM),
        scratch_shapes=[pltpu.VMEM((4, patch, patch), F32), pltpu.SemaphoreType.DMA((5,))],
        compiler_params=pltpu.CompilerParams(vmem_limit_bytes=8 * 2**20),
    )(returned, summed)


def solution(mesh):
    in_specs = (
        P(None, "contact", "tm"),
        P("contact", None),
        P(),
        P(),
        P(),
        P(),
        P(),
        P(),
        P(),
        P(None, "contact", "tm"),
    )
    out_specs = (P(None, "contact", "tm"), P())
    return jax.shard_map(local, mesh=mesh, in_specs=in_specs, out_specs=out_specs, check_vma=False)
```
